32 devices in a mesh: dev: 32 (over z, y, x, core).
Axes of the slice: x: 2, y: 2, z: 4, core: 2. Of those that a mesh axis runs over, the one named last changes fastest.
Arguments:
- embeddings: bfloat16 [32768, 128], P('dev'), may hold values from -6 to 6
- ranks: int32 [32768], P('dev'), may hold values from 0 to 32767, as said below
- pair_weight: bfloat16 [256, 128], replicated, may hold values from -0.375 to 0.375
- pair_bias: float32 [128], replicated, may hold values from -3 to 3
- score_weight: bfloat16 [128], replicated, may hold values from -0.5 to 0.5
Outputs:
- scores: float32 [31, 32768], P(None, 'dev')
The draws below stay inside these ranges and needn't reach their ends.
Inputs may be any that keep to these rules, and one draw needn't show every extreme that they name: ranks is a permutation of 0 .. 32767. Of the records of one device, at most 64 have ranks in any one range [o * 1024, (o + 1) * 1024); on every device some range holds exactly 64 of them, and every range holds exactly 64 of some device's records.
All inputs are finite; a program needn't handle non-finite values.
Results may differ from the reference program's by a relative error of at most 0.0045.
Values may be sent and summed in bfloat16 or wider, within the bound.
No kernel may reach another device: no remote copies, remote signals or barrier semaphores. Data moves between devices by JAX's collectives and lax.ppermute only.
A program may use at most 64 MiB of HBM per device.

```python
import jax
import jax.numpy as jnp
from jax import lax

E = 128
H = 128
WIN = 32
ROWS_DEV = 1024
NTOTAL = 32768


def draw_ranks(key, part):
    devices = NTOTAL // ROWS_DEV
    average = ROWS_DEV // devices
    base = jax.random.fold_in(key, 7919)
    key_owner, key_weight, key_rows, key_mix = jax.random.split(base, 4)
    owner_order = jax.random.permutation(key_owner, devices).astype(jnp.int32)
    halves = devices // 2 - 1
    lower = jax.random.randint(key_weight, (halves,), 0, 2 * average + 1).astype(jnp.int32)
    paired = jnp.stack([lower, 2 * average - lower], axis=1).reshape(-1)
    weights = jnp.concatenate([jnp.full((1,), 2 * average, jnp.int32), paired])
    bounds = jnp.cumsum(weights)
    slot_ids = jnp.arange(ROWS_DEV, dtype=jnp.int32)
    shifts = jnp.searchsorted(bounds, slot_ids, side='right').astype(jnp.int32)
    sources = jnp.arange(devices, dtype=jnp.int32)[:, None]
    owners = owner_order[(sources + shifts[None, :]) % devices]
    row_keys = jax.random.split(key_rows, devices)
    shuffles = jax.vmap(lambda one_key: jax.random.permutation(one_key, ROWS_DEV).astype(jnp.int32))(row_keys)
    owners = jnp.take_along_axis(owners, shuffles, axis=1)
    flat_owner = owners.reshape(-1)
    mixed = jax.random.permutation(key_mix, NTOTAL).astype(jnp.int32)
    placed = mixed[jnp.argsort(flat_owner[mixed], stable=True)]
    return jnp.zeros((NTOTAL,), jnp.int32).at[placed].set(jnp.arange(NTOTAL, dtype=jnp.int32))


def block_scale(key, shape, cuts, smallest, high):
    level, own = 1.0, jax.random.fold_in(key, 6)
    for dim, parts in cuts:
        heights = jnp.exp(jax.random.uniform(jax.random.fold_in(own, dim), (parts,), jnp.float32, smallest / len(cuts), high / len(cuts)))
        level = level * jnp.repeat(heights, shape[dim] // parts).reshape([-1 if axis == dim else 1 for axis in range(len(shape))])
    return level


def normal_values(key, shape, deviation, limit, pieces=(), kind=jnp.bfloat16):
    entries = deviation * jax.random.normal(key, shape, jnp.float32)
    if pieces:
        entries = entries * block_scale(key, shape, pieces, -0.22, 0.18)
    return jnp.clip(entries, -limit, limit).astype(kind)


def setup_inputs(seed: int = 0) -> dict:
    streams_of = jax.random.split(jax.random.key(seed), 6)
    embeddings = normal_values(streams_of[0], (NTOTAL, E), 1.0, 6.0, ((0, 32),))
    ranks = draw_ranks(jax.random.fold_in(streams_of[5], 71), 0)
    pair_weight = normal_values(streams_of[2], (2 * E, H), (2 * E) ** -0.5, 0.375)
    pair_bias = normal_values(streams_of[3], (H,), 0.5, 3.0, (), jnp.float32)
    score_weight = normal_values(streams_of[4], (H,), H ** -0.5, 0.5)
    return dict(embeddings=embeddings, ranks=ranks, pair_weight=pair_weight, pair_bias=pair_bias, score_weight=score_weight)


def reference(embeddings, ranks, pair_weight, pair_bias, score_weight):
    sorted_rows = jnp.zeros_like(embeddings).at[ranks].set(embeddings)
    padded = jnp.concatenate([sorted_rows, jnp.zeros((WIN - 1, E), embeddings.dtype)], axis=0)
    leading = sorted_rows.astype(jnp.float32)
    positions = jnp.arange(NTOTAL, dtype=jnp.int32)

    def one_offset(offset):
        partner = lax.dynamic_slice_in_dim(padded, offset, NTOTAL, 0).astype(jnp.float32)
        product = (leading * partner).astype(jnp.bfloat16)
        distance = jnp.abs(leading - partner).astype(jnp.bfloat16)
        features = jnp.concatenate([product, distance], axis=1)
        hidden = jnp.dot(features, pair_weight, preferred_element_type=jnp.float32) + pair_bias
        hidden = jax.nn.relu(hidden).astype(jnp.bfloat16)
        values = jnp.dot(hidden, score_weight, preferred_element_type=jnp.float32)
        return jnp.where(positions + offset < NTOTAL, values, jnp.zeros_like(values))

    offsets = jnp.arange(1, WIN, dtype=jnp.int32)
    return lax.map(one_offset, offsets)
```

```python
import functools

import jax
import jax.numpy as jnp
from jax import lax
from jax.experimental import pallas as pl
from jax.experimental.pallas import tpu as pltpu
from jax.sharding import PartitionSpec as P

WIN = 32
LANES = 128
CHUNK = 256
VMEM = pl.BlockSpec(memory_space=pltpu.VMEM)
SMEM = pl.BlockSpec(memory_space=pltpu.SMEM)


def one_hot(values, count):
    index = lax.broadcasted_iota(jnp.int32, (count, 1), 0).astype(jnp.float32)
    hit = values.astype(jnp.bfloat16) == index.astype(jnp.bfloat16)
    return jnp.where(hit, jnp.bfloat16(1), jnp.bfloat16(0))


def in_chunk(values, chunk):
    local = values - chunk * CHUNK
    return jnp.where((local >= 0) & (local < CHUNK), local, -1)


def pack_kernel(ranks_ref, rows_ref, out_ref, *, devices, capacity):
    count = rows_ref.shape[0]
    ranks = ranks_ref[...]
    owner = ranks // count
    position = ranks - owner * count
    high = (position // CHUNK + 1).astype(jnp.float32)
    low = (position % CHUNK).astype(jnp.float32)

    device_ids = lax.broadcasted_iota(jnp.int32, (devices, 1), 0)
    before = (
        lax.broadcasted_iota(jnp.int32, (CHUNK, CHUNK), 0)
        < lax.broadcasted_iota(jnp.int32, (CHUNK, CHUNK), 1)
    )
    before = jnp.where(before, 1.0, 0.0).astype(jnp.bfloat16)
    offset = jnp.zeros((devices, 1), jnp.float32)
    slots = []
    for start in range(0, count, CHUNK):
        member = jnp.where(device_ids == owner[:, start : start + CHUNK], 1.0, 0.0)
        earlier = jnp.dot(
            member.astype(jnp.bfloat16), before, preferred_element_type=jnp.float32
        )
        slots.append(jnp.sum(member * (earlier + offset), axis=0, keepdims=True))
        offset = offset + jnp.sum(member, axis=1, keepdims=True)
    slot = jnp.concatenate(slots, axis=1)
    target = owner * capacity + slot.astype(jnp.int32)

    rows = rows_ref[...]
    group = CHUNK // capacity
    for chunk in range(devices * capacity // CHUNK):
        pick = one_hot(in_chunk(target, chunk), CHUNK)
        packed = jnp.dot(pick, rows, preferred_element_type=jnp.float32)
        out_ref[chunk * group : (chunk + 1) * group, :capacity, :] = packed.reshape(
            group, capacity, LANES
        ).astype(jnp.bfloat16)

    lane = lax.broadcasted_iota(jnp.int32, (LANES, 1), 0) % capacity
    spot = jnp.where(slot.astype(jnp.int32) == lane, 1.0, 0.0).astype(jnp.bfloat16)
    line = lax.broadcasted_iota(jnp.int32, (devices * 8, 1), 0)
    kind = line % 8
    value = jnp.where(kind == 0, high, jnp.where(kind == 1, low, 0.0))
    value = jnp.where(line // 8 == owner, value, 0.0).astype(jnp.bfloat16)
    places = lax.dot_general(
        value, spot, (((1,), (1,)), ((), ())), preferred_element_type=jnp.float32
    )
    out_ref[:, capacity:, :] = places.reshape(devices, 8, LANES).astype(jnp.bfloat16)


def sort_kernel(arrived_ref, wide_ref, narrow_ref, head_ref, *, capacity):
    devices = arrived_ref.shape[0]
    share = LANES // capacity
    lane = lax.broadcasted_iota(jnp.int32, (8, LANES), 1)
    highs, lows = [], []
    for first in range(0, devices, share):
        places = arrived_ref[first, capacity:, :].astype(jnp.float32)
        for step in range(1, share):
            other = arrived_ref[first + step, capacity:, :].astype(jnp.float32)
            places = jnp.where(lane >= step * capacity, other, places)
        highs.append(places[0:1])
        lows.append(places[1:2])
    high = jnp.concatenate(highs, axis=1)
    low = jnp.concatenate(lows, axis=1)
    rows = arrived_ref[:, :capacity, :].reshape(devices * capacity, LANES)
    for chunk in range(wide_ref.shape[0] // CHUNK):
        pick = one_hot(jnp.where(high == chunk + 1, low, -1.0), CHUNK)
        ordered = jnp.dot(pick, rows, preferred_element_type=jnp.float32)
        wide_ref[chunk * CHUNK : (chunk + 1) * CHUNK, :] = ordered
        narrow_ref[chunk * CHUNK : (chunk + 1) * CHUNK, :] = ordered.astype(jnp.bfloat16)
        if chunk == 0:
            head_ref[...] = ordered[:WIN].astype(jnp.bfloat16)


def score_block(leading, wide_ref, start, offset, weight, bias_ref, score_ref):
    partner = wide_ref[pl.ds(start + offset, CHUNK), :].astype(jnp.bfloat16)
    features = jnp.concatenate([leading * partner, jnp.abs(leading - partner)], axis=1)
    hidden = lax.dot_general(
        weight, features, (((1,), (1,)), ((), ())), preferred_element_type=jnp.float32
    )
    hidden = jnp.maximum(hidden + bias_ref[...], 0.0) * score_ref[...]
    return jnp.sum(hidden, axis=0, keepdims=True)


def main_kernel(wide_ref, narrow_ref, weight_ref, bias_ref, score_ref, out_ref):
    weight = weight_ref[...]

    def step(offset, carry):
        for start in range(0, out_ref.shape[1], CHUNK):
            leading = narrow_ref[start : start + CHUNK, :]
            out_ref[pl.ds(offset - 1, 1), start : start + CHUNK] = score_block(
                leading, wide_ref, start, offset, weight, bias_ref, score_ref
            )
        return carry

    lax.fori_loop(1, WIN, step, 0)


def tail_kernel(
    limit_ref, wide_ref, narrow_ref, next_ref, weight_ref, bias_ref, score_ref, _, out_ref,
    joined_ref,
):
    weight = weight_ref[...]
    count = wide_ref.shape[0]
    base = count - CHUNK
    joined_ref[:CHUNK, :] = wide_ref[base:, :]
    joined_ref[CHUNK:, :] = next_ref[...].astype(jnp.float32)
    leading = narrow_ref[base:, :]
    place = base + lax.broadcasted_iota(jnp.int32, (1, CHUNK), 1)
    limit = limit_ref[0]

    def step(offset, carry):
        line = score_block(leading, joined_ref, 0, offset, weight, bias_ref, score_ref)
        out_ref[pl.ds(offset - 1, 1), :] = jnp.where(place + offset < limit, line, 0.0)
        return carry

    lax.fori_loop(1, WIN, step, 0)


def body(embeddings, ranks, pair_weight, pair_bias, score_weight):
    rows_dev, width = embeddings.shape
    devices = lax.axis_size("dev")
    capacity = 2 * rows_dev // devices
    hidden = pair_weight.shape[1]

    outgoing = pl.pallas_call(
        functools.partial(pack_kernel, devices=devices, capacity=capacity),
        out_shape=jax.ShapeDtypeStruct((devices, capacity + 8, width), jnp.bfloat16),
        in_specs=[VMEM] * 2,
        out_specs=VMEM,
        name="pack",
    )(ranks.reshape(1, rows_dev), embeddings)
    arrived = lax.all_to_all(outgoing, "dev", split_axis=0, concat_axis=0, tiled=True)
    weight = pair_weight.T
    bias = jnp.broadcast_to(pair_bias[:, None], (hidden, CHUNK))
    score = jnp.broadcast_to(score_weight.astype(jnp.float32)[:, None], (hidden, CHUNK))

    wide, narrow, head = pl.pallas_call(
        functools.partial(sort_kernel, capacity=capacity),
        out_shape=(
            jax.ShapeDtypeStruct((rows_dev, width), jnp.float32),
            jax.ShapeDtypeStruct((rows_dev, width), jnp.bfloat16),
            jax.ShapeDtypeStruct((WIN, width), jnp.bfloat16),
        ),
        in_specs=[VMEM],
        out_specs=(VMEM, VMEM, VMEM),
        name="sort",
    )(arrived)
    following = lax.ppermute(head, "dev", [(i, i - 1) for i in range(1, devices)])

    pairs = (WIN - 1) * rows_dev
    scores = pl.pallas_call(
        main_kernel,
        grid=(1,),
        out_shape=jax.ShapeDtypeStruct((WIN - 1, rows_dev), jnp.float32),
        in_specs=[VMEM] * 5,
        out_specs=pl.BlockSpec((WIN - 1, rows_dev - CHUNK), lambda i: (0, 0)),
        cost_estimate=pl.CostEstimate(
            flops=4 * pairs * width * hidden, bytes_accessed=4 * pairs, transcendentals=0
        ),
        name="main",
    )(wide, narrow, weight, bias, score)
    last = lax.axis_index("dev") == devices - 1
    limit = jnp.where(last, rows_dev, 2 * rows_dev).astype(jnp.int32).reshape(1)
    return pl.pallas_call(
        tail_kernel,
        grid=(1,),
        out_shape=jax.ShapeDtypeStruct((WIN - 1, rows_dev), jnp.float32),
        in_specs=[SMEM] + [VMEM] * 6 + [pl.BlockSpec(memory_space=pl.ANY)],
        out_specs=pl.BlockSpec((WIN - 1, CHUNK), lambda i: (0, rows_dev // CHUNK - 1)),
        scratch_shapes=[pltpu.VMEM((CHUNK + WIN, width), jnp.float32)],
        input_output_aliases={7: 0},
        name="tail",
    )(limit, wide, narrow, following, weight, bias, score, scores)


def solution(mesh):
    placed = (P("dev", None), P("dev"), P(), P(), P())
    return jax.shard_map(
        body, mesh=mesh, in_specs=placed, out_specs=P(None, "dev"), check_vma=False
    )
```

```python
import functools

import jax
import jax.numpy as jnp
from jax import lax
from jax.experimental import pallas as pl
from jax.experimental.pallas import tpu as pltpu
from jax.sharding import PartitionSpec as P

WIN = 32
LANES = 128
CHUNK = 256
VMEM = pl.BlockSpec(memory_space=pltpu.VMEM)
SMEM = pl.BlockSpec(memory_space=pltpu.SMEM)
ANY = pl.BlockSpec(memory_space=pl.ANY)
SMALL = pltpu.CompilerParams(vmem_limit_bytes=16 * 2**20)


def one_hot(values, count):
    index = lax.broadcasted_iota(jnp.int32, (count, 1), 0).astype(jnp.float32)
    hit = values.astype(jnp.bfloat16) == index.astype(jnp.bfloat16)
    return jnp.where(hit, jnp.bfloat16(1), jnp.bfloat16(0))


def in_chunk(values, chunk):
    local = values - chunk * CHUNK
    return jnp.where((local >= 0) & (local < CHUNK), local, -1)


def pack_kernel(ranks_ref, rows_ref, out_ref, *, devices, capacity):
    count = rows_ref.shape[0]
    ranks = ranks_ref[...]
    owner = ranks // count
    position = ranks - owner * count
    high = (position // CHUNK + 1).astype(jnp.float32)
    low = (position % CHUNK).astype(jnp.float32)

    device_ids = lax.broadcasted_iota(jnp.int32, (devices, 1), 0)
    before = (
        lax.broadcasted_iota(jnp.int32, (CHUNK, CHUNK), 0)
        < lax.broadcasted_iota(jnp.int32, (CHUNK, CHUNK), 1)
    )
    before = jnp.where(before, 1.0, 0.0).astype(jnp.bfloat16)
    offset = jnp.zeros((devices, 1), jnp.float32)
    slots = []
    for start in range(0, count, CHUNK):
        member = jnp.where(device_ids == owner[:, start : start + CHUNK], 1.0, 0.0)
        earlier = jnp.dot(
            member.astype(jnp.bfloat16), before, preferred_element_type=jnp.float32
        )
        slots.append(jnp.sum(member * (earlier + offset), axis=0, keepdims=True))
        offset = offset + jnp.sum(member, axis=1, keepdims=True)
    slot = jnp.concatenate(slots, axis=1)
    target = owner * capacity + slot.astype(jnp.int32)

    rows = rows_ref[...]
    group = CHUNK // capacity
    for chunk in range(devices * capacity // CHUNK):
        pick = one_hot(in_chunk(target, chunk), CHUNK)
        packed = jnp.dot(pick, rows, preferred_element_type=jnp.float32)
        out_ref[chunk * group : (chunk + 1) * group, :capacity, :] = packed.reshape(
            group, capacity, LANES
        ).astype(jnp.bfloat16)

    lane = lax.broadcasted_iota(jnp.int32, (LANES, 1), 0) % capacity
    spot = jnp.where(slot.astype(jnp.int32) == lane, 1.0, 0.0).astype(jnp.bfloat16)
    line = lax.broadcasted_iota(jnp.int32, (devices * 8, 1), 0)
    kind = line % 8
    value = jnp.where(kind == 0, high, jnp.where(kind == 1, low, 0.0))
    value = jnp.where(line // 8 == owner, value, 0.0).astype(jnp.bfloat16)
    places = lax.dot_general(
        value, spot, (((1,), (1,)), ((), ())), preferred_element_type=jnp.float32
    )
    out_ref[:, capacity:, :] = places.reshape(devices, 8, LANES).astype(jnp.bfloat16)


def sort_kernel(arrived_ref, *refs, capacity):
    wide_ref, head_ref = refs[-2:]
    devices = arrived_ref.shape[0]
    share = LANES // capacity
    lane = lax.broadcasted_iota(jnp.int32, (8, LANES), 1)
    highs, lows = [], []
    for first in range(0, devices, share):
        places = arrived_ref[first, capacity:, :].astype(jnp.float32)
        for step in range(1, share):
            other = arrived_ref[first + step, capacity:, :].astype(jnp.float32)
            places = jnp.where(lane >= step * capacity, other, places)
        highs.append(places[0:1])
        lows.append(places[1:2])
    high = jnp.concatenate(highs, axis=1)
    low = jnp.concatenate(lows, axis=1)
    rows = arrived_ref[:, :capacity, :].reshape(devices * capacity, LANES)
    for chunk in range(wide_ref.shape[0] // CHUNK):
        pick = one_hot(jnp.where(high == chunk + 1, low, -1.0), CHUNK)
        ordered = jnp.dot(pick, rows, preferred_element_type=jnp.float32)
        wide_ref[chunk * CHUNK : (chunk + 1) * CHUNK, :] = ordered
        if chunk == 0:
            head_ref[...] = ordered[:WIN].astype(jnp.bfloat16)


def prepare_kernel(weight_ref, bias_ref, score_ref, turned_ref, floor_ref, scale_ref, base_ref):
    turned_ref[...] = weight_ref[...].astype(jnp.float32).T.astype(jnp.bfloat16)
    bias = bias_ref[...]
    score = score_ref[...].astype(jnp.float32)
    hidden = bias.shape[1]
    floor = jnp.broadcast_to(-bias, (CHUNK, hidden)).T
    floor_ref[...] = floor
    scale_ref[...] = jnp.broadcast_to(score, (CHUNK, hidden)).T
    base_ref[...] = jnp.broadcast_to(
        jnp.sum(bias * score, axis=1, keepdims=True), base_ref.shape
    )


def score_tile(leading, partner, weight, floor_ref, scale_ref, base_ref):
    features = jnp.concatenate([leading * partner, jnp.abs(leading - partner)], axis=1)
    hidden = lax.dot_general(
        weight, features, (((1,), (1,)), ((), ())), preferred_element_type=jnp.float32
    )
    hidden = jnp.maximum(hidden, floor_ref[...]) * scale_ref[...]
    return jnp.sum(hidden, axis=0, keepdims=True) + base_ref[...]


def score_blocks(blocks, wide_ref, write, parameters):
    weight = parameters[0][...]
    half = WIN // 2
    leadings = [wide_ref[b * CHUNK : (b + 1) * CHUNK, :].astype(jnp.bfloat16) for b in range(blocks)]
    for offset in range(1, half + 1):
        for b in range(blocks):
            first = b * CHUNK + offset
            extra = half if offset < half else 0
            partner = wide_ref[first : first + CHUNK + extra, :].astype(jnp.bfloat16)
            for add in (0, half)[: 2 if extra else 1]:
                line = score_tile(
                    leadings[b], partner[add : add + CHUNK], weight, *parameters[1:]
                )
                write(offset + add, b, line)


def main_kernel(wide_ref, turned_ref, floor_ref, scale_ref, base_ref, out_ref):
    def write(offset, block, line):
        out_ref[offset - 1 : offset, block * CHUNK : (block + 1) * CHUNK] = line

    score_blocks(
        out_ref.shape[1] // CHUNK, wide_ref, write, (turned_ref, floor_ref, scale_ref, base_ref)
    )


def tail_kernel(
    limit_ref, wide_ref, next_ref, turned_ref, floor_ref, scale_ref, base_ref, _, out_ref,
    joined_ref,
):
    count = wide_ref.shape[0]
    joined_ref[:CHUNK, :] = wide_ref[count - CHUNK :, :]
    joined_ref[CHUNK:, :] = next_ref[...].astype(jnp.float32)
    place = count - CHUNK + lax.broadcasted_iota(jnp.int32, (1, CHUNK), 1)
    limit = limit_ref[0]

    def write(offset, block, line):
        out_ref[offset - 1 : offset, :] = jnp.where(place + offset < limit, line, 0.0)

    score_blocks(1, joined_ref, write, (turned_ref, floor_ref, scale_ref, base_ref))


def body(embeddings, ranks, pair_weight, pair_bias, score_weight):
    rows_dev, width = embeddings.shape
    devices = lax.axis_size("dev")
    capacity = 2 * rows_dev // devices
    hidden = pair_weight.shape[1]

    outgoing = pl.pallas_call(
        functools.partial(pack_kernel, devices=devices, capacity=capacity),
        out_shape=jax.ShapeDtypeStruct((devices, capacity + 8, width), jnp.bfloat16),
        in_specs=[VMEM] * 2,
        out_specs=VMEM,
        compiler_params=SMALL,
        name="pack",
    )(ranks.reshape(1, rows_dev), embeddings)
    arrived = lax.all_to_all(outgoing, "dev", split_axis=0, concat_axis=0, tiled=True)
    parameters = pl.pallas_call(
        prepare_kernel,
        out_shape=(
            jax.ShapeDtypeStruct((hidden, 2 * width), jnp.bfloat16),
            jax.ShapeDtypeStruct((hidden, CHUNK), jnp.float32),
            jax.ShapeDtypeStruct((hidden, CHUNK), jnp.float32),
            jax.ShapeDtypeStruct((1, CHUNK), jnp.float32),
        ),
        in_specs=[VMEM] * 3,
        out_specs=(VMEM,) * 4,
        compiler_params=SMALL,
        name="prepare",
    )(pair_weight, pair_bias.reshape(1, hidden), score_weight.reshape(1, hidden))

    wide, head = pl.pallas_call(
        functools.partial(sort_kernel, capacity=capacity),
        out_shape=(
            jax.ShapeDtypeStruct((rows_dev, width), jnp.float32),
            jax.ShapeDtypeStruct((WIN, width), jnp.bfloat16),
        ),
        in_specs=[VMEM] + [ANY] * 4,
        out_specs=(VMEM, VMEM),
        compiler_params=SMALL,
        name="sort",
    )(arrived, *parameters)
    following = lax.ppermute(head, "dev", [(i, i - 1) for i in range(1, devices)])

    pairs = (WIN - 1) * (rows_dev - CHUNK)
    scores = pl.pallas_call(
        main_kernel,
        grid=(1,),
        out_shape=jax.ShapeDtypeStruct((WIN - 1, rows_dev), jnp.float32),
        in_specs=[VMEM] * 5,
        out_specs=pl.BlockSpec((WIN - 1, rows_dev - CHUNK), lambda i: (0, 0)),
        cost_estimate=pl.CostEstimate(
            flops=4 * pairs * width * hidden, bytes_accessed=4 * pairs, transcendentals=0
        ),
        compiler_params=SMALL,
        name="main",
    )(wide, *parameters)
    last = lax.axis_index("dev") == devices - 1
    limit = jnp.where(last, rows_dev, 2 * rows_dev).astype(jnp.int32).reshape(1)
    return pl.pallas_call(
        tail_kernel,
        grid=(1,),
        out_shape=jax.ShapeDtypeStruct((WIN - 1, rows_dev), jnp.float32),
        in_specs=[SMEM] + [VMEM] * 6 + [ANY],
        out_specs=pl.BlockSpec((WIN - 1, CHUNK), lambda i: (0, rows_dev // CHUNK - 1)),
        scratch_shapes=[pltpu.VMEM((CHUNK + WIN, width), jnp.float32)],
        input_output_aliases={7: 0},
        compiler_params=SMALL,
        name="tail",
    )(limit, wide, following, *parameters, scores)


def solution(mesh):
    placed = (P("dev", None), P("dev"), P(), P(), P())
    return jax.shard_map(
        body, mesh=mesh, in_specs=placed, out_specs=P(None, "dev"), check_vma=False
    )
```

```python
import functools

import jax
import jax.numpy as jnp
from jax import lax
from jax.experimental import pallas as pl
from jax.experimental.pallas import tpu as pltpu
from jax.sharding import PartitionSpec as P

WIN = 32
LANES = 128
CHUNK = 256
VMEM = pl.BlockSpec(memory_space=pltpu.VMEM)
SMEM = pl.BlockSpec(memory_space=pltpu.SMEM)
ANY = pl.BlockSpec(memory_space=pl.ANY)
SMALL = pltpu.CompilerParams(vmem_limit_bytes=16 * 2**20)


def one_hot(values, count):
    index = lax.broadcasted_iota(jnp.int32, (count, 1), 0).astype(jnp.float32)
    hit = values.astype(jnp.bfloat16) == index.astype(jnp.bfloat16)
    return jnp.where(hit, jnp.bfloat16(1), jnp.bfloat16(0))


def in_chunk(values, chunk):
    local = values - chunk * CHUNK
    return jnp.where((local >= 0) & (local < CHUNK), local, -1)


def pack_kernel(ranks_hbm, rows_hbm, out_ref, ranks_ref, rows_ref, sems, *, devices, capacity):
    ranks_copy = pltpu.make_async_copy(ranks_hbm, ranks_ref, sems.at[0])
    rows_copy = pltpu.make_async_copy(rows_hbm, rows_ref, sems.at[1])
    ranks_copy.start()
    rows_copy.start()
    count = rows_ref.shape[0]
    ranks_copy.wait()
    ranks = ranks_ref[...]
    owner = ranks // count
    position = ranks - owner * count
    high = (position // CHUNK + 1).astype(jnp.float32)
    low = (position % CHUNK).astype(jnp.float32)

    device_ids = lax.broadcasted_iota(jnp.int32, (devices, 1), 0)
    before = (
        lax.broadcasted_iota(jnp.int32, (CHUNK, CHUNK), 0)
        < lax.broadcasted_iota(jnp.int32, (CHUNK, CHUNK), 1)
    )
    before = jnp.where(before, 1.0, 0.0).astype(jnp.bfloat16)
    offset = jnp.zeros((devices, 1), jnp.float32)
    slots = []
    for start in range(0, count, CHUNK):
        member = jnp.where(device_ids == owner[:, start : start + CHUNK], 1.0, 0.0)
        earlier = jnp.dot(
            member.astype(jnp.bfloat16), before, preferred_element_type=jnp.float32
        )
        slots.append(jnp.sum(member * (earlier + offset), axis=0, keepdims=True))
        offset = offset + jnp.sum(member, axis=1, keepdims=True)
    slot = jnp.concatenate(slots, axis=1)
    target = owner * capacity + slot.astype(jnp.int32)

    rows_copy.wait()
    rows = rows_ref[...]
    group = CHUNK // capacity
    for chunk in range(devices * capacity // CHUNK):
        pick = one_hot(in_chunk(target, chunk), CHUNK)
        packed = jnp.dot(pick, rows, preferred_element_type=jnp.float32)
        out_ref[chunk * group : (chunk + 1) * group, :capacity, :] = packed.reshape(
            group, capacity, LANES
        ).astype(jnp.bfloat16)

    lane = lax.broadcasted_iota(jnp.int32, (LANES, 1), 0) % capacity
    spot = jnp.where(slot.astype(jnp.int32) == lane, 1.0, 0.0).astype(jnp.bfloat16)
    line = lax.broadcasted_iota(jnp.int32, (devices * 8, 1), 0)
    kind = line % 8
    value = jnp.where(kind == 0, high, jnp.where(kind == 1, low, 0.0))
    value = jnp.where(line // 8 == owner, value, 0.0).astype(jnp.bfloat16)
    places = lax.dot_general(
        value, spot, (((1,), (1,)), ((), ())), preferred_element_type=jnp.float32
    )
    out_ref[:, capacity:, :] = places.reshape(devices, 8, LANES).astype(jnp.bfloat16)


def ordered_chunks(arrived_ref, count, capacity):
    devices = arrived_ref.shape[0]
    share = LANES // capacity
    lane = lax.broadcasted_iota(jnp.int32, (8, LANES), 1)
    highs, lows = [], []
    for first in range(0, devices, share):
        places = arrived_ref[first, capacity:, :].astype(jnp.float32)
        for step in range(1, share):
            other = arrived_ref[first + step, capacity:, :].astype(jnp.float32)
            places = jnp.where(lane >= step * capacity, other, places)
        highs.append(places[0:1])
        lows.append(places[1:2])
    high = jnp.concatenate(highs, axis=1)
    low = jnp.concatenate(lows, axis=1)
    rows = arrived_ref[:, :capacity, :].reshape(devices * capacity, LANES)
    for chunk in range(count // CHUNK):
        pick = one_hot(jnp.where(high == chunk + 1, low, -1.0), CHUNK)
        yield jnp.dot(pick, rows, preferred_element_type=jnp.float32)


def prepare_kernel(weight_ref, bias_ref, score_ref, turned_ref, floor_ref, scale_ref, base_ref):
    turned_ref[...] = weight_ref[...].astype(jnp.float32).T.astype(jnp.bfloat16)
    bias = bias_ref[...]
    score = score_ref[...].astype(jnp.float32)
    hidden = bias.shape[1]
    floor = jnp.broadcast_to(-bias, (CHUNK, hidden)).T
    floor_ref[...] = floor
    scale_ref[...] = jnp.broadcast_to(score, (CHUNK, hidden)).T
    base_ref[...] = jnp.broadcast_to(
        jnp.sum(bias * score, axis=1, keepdims=True), base_ref.shape
    )


def score_block(columns, write, turned_ref, floor_ref, scale_ref, base_ref):
    columns = columns.astype(jnp.bfloat16)
    leading = columns[:, :CHUNK]
    weight = turned_ref[...]
    for offset in range(1, WIN):
        partner = pltpu.roll(columns, columns.shape[1] - offset, 1)[:, :CHUNK]
        features = jnp.concatenate(
            [leading * partner, jnp.abs(leading - partner)], axis=0
        )
        hidden = jnp.dot(weight, features, preferred_element_type=jnp.float32)
        hidden = jnp.maximum(hidden, floor_ref[...]) * scale_ref[...]
        write(offset, jnp.sum(hidden, axis=0, keepdims=True) + base_ref[...])


def score_inner(wide_ref, out_ref, first, parameters):
    for block in range(out_ref.shape[1] // CHUNK):
        start = (first + block) * CHUNK

        def write(offset, line, place=block * CHUNK):
            out_ref[offset - 1 : offset, place : place + CHUNK] = line

        score_block(wide_ref[:, start : start + CHUNK + LANES], write, *parameters)


def sort_kernel(arrived_ref, *refs, capacity):
    parameters, (wide_ref, head_ref, out_ref) = refs[:4], refs[4:]
    for chunk, ordered in enumerate(ordered_chunks(arrived_ref, wide_ref.shape[1], capacity)):
        wide_ref[:, chunk * CHUNK : (chunk + 1) * CHUNK] = ordered.T
        if chunk == 0:
            head_ref[...] = ordered[: head_ref.shape[0]].astype(jnp.bfloat16)
    score_inner(wide_ref, out_ref, 0, parameters)


def middle_kernel(wide_ref, *refs, first):
    score_inner(wide_ref, refs[4], first, refs[:4])


def tail_kernel(
    limit_ref, wide_ref, next_ref, turned_ref, floor_ref, scale_ref, base_ref,
    early_ref, middle_ref, out_ref, late_ref, sems,
):
    count = wide_ref.shape[1]
    base = count - CHUNK
    split = early_ref.shape[1]
    copies = [
        pltpu.make_async_copy(early_ref, out_ref.at[:, :split], sems.at[0]),
        pltpu.make_async_copy(middle_ref, out_ref.at[:, split:base], sems.at[1]),
    ]
    for copy in copies:
        copy.start()
    following = next_ref[...].astype(jnp.float32)
    padding = jnp.zeros((LANES - following.shape[0], LANES), jnp.float32)
    following = jnp.concatenate([following, padding], axis=0).T
    columns = jnp.concatenate([wide_ref[:, base:], following], axis=1)
    place = base + lax.broadcasted_iota(jnp.int32, (1, CHUNK), 1)
    limit = limit_ref[0]

    def write(offset, line):
        late_ref[offset - 1 : offset, :] = jnp.where(place + offset < limit, line, 0.0)

    score_block(columns, write, turned_ref, floor_ref, scale_ref, base_ref)
    last = pltpu.make_async_copy(late_ref, out_ref.at[:, base:], sems.at[2])
    last.start()
    for copy in copies:
        copy.wait()
    last.wait()


def body(embeddings, ranks, pair_weight, pair_bias, score_weight):
    rows_dev, width = embeddings.shape
    devices = lax.axis_size("dev")
    capacity = 2 * rows_dev // devices
    hidden = pair_weight.shape[1]

    outgoing = pl.pallas_call(
        functools.partial(pack_kernel, devices=devices, capacity=capacity),
        out_shape=jax.ShapeDtypeStruct((devices, capacity + 8, width), jnp.bfloat16),
        in_specs=[ANY] * 2,
        out_specs=VMEM,
        scratch_shapes=[
            pltpu.VMEM((1, rows_dev), jnp.int32),
            pltpu.VMEM((rows_dev, width), jnp.bfloat16),
            pltpu.SemaphoreType.DMA((2,)),
        ],
        name="pack",
    )(ranks.reshape(1, rows_dev), embeddings)
    arrived = lax.all_to_all(outgoing, "dev", split_axis=0, concat_axis=0, tiled=True)
    parameters = pl.pallas_call(
        prepare_kernel,
        out_shape=(
            jax.ShapeDtypeStruct((hidden, 2 * width), jnp.bfloat16),
            jax.ShapeDtypeStruct((hidden, CHUNK), jnp.float32),
            jax.ShapeDtypeStruct((hidden, CHUNK), jnp.float32),
            jax.ShapeDtypeStruct((1, CHUNK), jnp.float32),
        ),
        in_specs=[VMEM] * 3,
        out_specs=(VMEM,) * 4,
        compiler_params=SMALL,
        name="prepare",
    )(pair_weight, pair_bias.reshape(1, hidden), score_weight.reshape(1, hidden))

    def cost(columns):
        pairs = (WIN - 1) * columns
        return pl.CostEstimate(
            flops=4 * pairs * width * hidden, bytes_accessed=4 * pairs, transcendentals=0
        )

    early = CHUNK
    middle = rows_dev - 2 * CHUNK
    wide, head, scores_early = pl.pallas_call(
        functools.partial(sort_kernel, capacity=capacity),
        out_shape=(
            jax.ShapeDtypeStruct((width, rows_dev), jnp.float32),
            jax.ShapeDtypeStruct((WIN, width), jnp.bfloat16),
            jax.ShapeDtypeStruct((WIN - 1, early), jnp.float32),
        ),
        in_specs=[VMEM] * 5,
        out_specs=(VMEM,) * 3,
        cost_estimate=cost(early),
        compiler_params=SMALL,
        name="sort",
    )(arrived, *parameters)
    following = lax.ppermute(head, "dev", [(i, i - 1) for i in range(1, devices)])
    scores_middle = pl.pallas_call(
        functools.partial(middle_kernel, first=early // CHUNK),
        out_shape=jax.ShapeDtypeStruct((WIN - 1, middle), jnp.float32),
        in_specs=[VMEM] * 5,
        out_specs=VMEM,
        cost_estimate=cost(middle),
        compiler_params=SMALL,
        name="middle",
    )(wide, *parameters)
    last = lax.axis_index("dev") == devices - 1
    limit = jnp.where(last, rows_dev, 2 * rows_dev).astype(jnp.int32).reshape(1)
    return pl.pallas_call(
        tail_kernel,
        out_shape=jax.ShapeDtypeStruct((WIN - 1, rows_dev), jnp.float32),
        in_specs=[SMEM] + [VMEM] * 8,
        out_specs=ANY,
        scratch_shapes=[
            pltpu.VMEM((WIN - 1, CHUNK), jnp.float32),
            pltpu.SemaphoreType.DMA((3,)),
        ],
        cost_estimate=cost(CHUNK),
        compiler_params=SMALL,
        name="tail",
    )(limit, wide, following, *parameters, scores_early, scores_middle)


def solution(mesh):
    placed = (P("dev", None), P("dev"), P(), P(), P())
    return jax.shard_map(
        body, mesh=mesh, in_specs=placed, out_specs=P(None, "dev"), check_vma=False
    )
```

```python
import functools

import jax
import jax.numpy as jnp
from jax import lax
from jax.experimental import pallas as pl
from jax.experimental.pallas import tpu as pltpu
from jax.sharding import PartitionSpec as P

WIN = 32
LANES = 128
CHUNK = 256
SPARE = 6
LOST = 255.0
VMEM = pl.BlockSpec(memory_space=pltpu.VMEM)
SMEM = pl.BlockSpec(memory_space=pltpu.SMEM)
ANY = pl.BlockSpec(memory_space=pl.ANY)
HBM = pl.BlockSpec(memory_space=pltpu.HBM)
SMALL = pltpu.CompilerParams(vmem_limit_bytes=16 * 2**20)


def matches(values, count):
    index = lax.broadcasted_iota(jnp.int32, (count, 1), 0).astype(jnp.float32)
    return values.astype(jnp.bfloat16) == index.astype(jnp.bfloat16)


def one_hot(values, count):
    return jnp.where(matches(values, count), jnp.bfloat16(1), jnp.bfloat16(0))


def in_chunk(values, chunk):
    local = values - chunk * CHUNK
    return jnp.where((local >= 0) & (local < CHUNK), local, -1)


def pack_kernel(
    me_ref, ranks_hbm, rows_hbm, out_ref, ranks_ref, rows_ref, sems, *, devices, capacity
):
    ranks_copy = pltpu.make_async_copy(ranks_hbm, ranks_ref, sems.at[0])
    rows_copy = pltpu.make_async_copy(rows_hbm, rows_ref, sems.at[1])
    ranks_copy.start()
    rows_copy.start()
    count = rows_ref.shape[0]
    ranks_copy.wait()
    ranks = ranks_ref[...]
    owner = ranks // count
    position = ranks - owner * count
    before_owner = jnp.where(position < WIN - 1, owner, 0) - 1

    device_ids = lax.broadcasted_iota(jnp.int32, (devices, 1), 0)
    before = (
        lax.broadcasted_iota(jnp.int32, (CHUNK, CHUNK), 0)
        < lax.broadcasted_iota(jnp.int32, (CHUNK, CHUNK), 1)
    )
    before = jnp.where(before, 1.0, 0.0).astype(jnp.bfloat16)
    totals = jnp.zeros((2 * devices, 1), jnp.float32)
    members, indices = [], []
    for start in range(0, count, CHUNK):
        span = slice(start, start + CHUNK)
        member = jnp.concatenate(
            [
                jnp.where(device_ids == owner[:, span], 1.0, 0.0),
                jnp.where(device_ids == before_owner[:, span], 1.0, 0.0),
            ],
            axis=0,
        )
        earlier = jnp.dot(
            member.astype(jnp.bfloat16), before, preferred_element_type=jnp.float32
        )
        members.append(member)
        indices.append(earlier + totals)
        totals = totals + jnp.sum(member, axis=1, keepdims=True)
    owned = totals[:devices]
    slot = jnp.concatenate(
        [
            jnp.sum(m[:devices] * i[:devices], axis=0, keepdims=True)
            for m, i in zip(members, indices)
        ],
        axis=1,
    ).astype(jnp.int32)
    again = jnp.concatenate(
        [
            jnp.sum(m[devices:] * (i[devices:] + owned), axis=0, keepdims=True)
            for m, i in zip(members, indices)
        ],
        axis=1,
    ).astype(jnp.int32)
    extra = before_owner >= 0
    fits = extra & (again < capacity)
    spare = extra & (again >= capacity) & (again < capacity + SPARE)
    lost = jnp.where(extra & (again >= capacity + SPARE), 1.0, 0.0)
    target = owner * capacity + slot
    second = jnp.where(fits, before_owner * capacity + again, -1)
    third = jnp.where(spare, before_owner * 8 + (again - capacity + 8 - SPARE), -1)

    high = (position // CHUNK + 1).astype(jnp.float32)
    low = (position % CHUNK).astype(jnp.float32)
    head = position.astype(jnp.float32)
    lane = lax.broadcasted_iota(jnp.int32, (LANES, 1), 0)
    corner = (me_ref[0] % (LANES // 8)) * 8
    spot = jnp.where(slot == lane % capacity, 1.0, 0.0).astype(jnp.bfloat16)
    where_again = jnp.where(
        fits, again, jnp.where(spare, LANES + corner + again - capacity + 8 - SPARE, -1)
    )
    spot_again = jnp.where(
        (where_again == lane % capacity) | (where_again == LANES + lane), 1.0, 0.0
    ).astype(jnp.bfloat16)
    mine = device_ids == owner
    theirs = device_ids == before_owner
    values = jnp.concatenate(
        [
            jnp.where(mine, high, 0.0),
            jnp.where(mine, low, 0.0),
            jnp.zeros((devices, count), jnp.float32),
        ],
        axis=0,
    ).astype(jnp.bfloat16)
    values_again = jnp.concatenate(
        [
            jnp.where(theirs & fits, jnp.float32(count // CHUNK + 1), 0.0),
            jnp.where(theirs & fits, head, 0.0),
            jnp.where(theirs & spare, head + 1.0, 0.0),
        ],
        axis=0,
    ).astype(jnp.bfloat16)
    contract = (((1,), (1,)), ((), ()))
    places = lax.dot_general(
        values, spot, contract, preferred_element_type=jnp.float32
    ) + lax.dot_general(
        values_again, spot_again, contract, preferred_element_type=jnp.float32
    )
    lane_row = lax.broadcasted_iota(jnp.int32, (1, LANES), 1)
    main_line = jnp.where(
        lane_row < capacity, places[:devices], places[devices : 2 * devices]
    )
    lost = jnp.max(lost, axis=1, keepdims=True)
    spare_line = places[2 * devices :] + jnp.where(lane_row == corner, LOST * lost, 0.0)

    rows_copy.wait()
    rows = rows_ref[...]
    group = CHUNK // capacity
    for chunk in range(devices * capacity // CHUNK):
        pick = jnp.where(
            matches(in_chunk(target, chunk), CHUNK) | matches(in_chunk(second, chunk), CHUNK),
            jnp.bfloat16(1),
            jnp.bfloat16(0),
        )
        packed = jnp.dot(pick, rows, preferred_element_type=jnp.float32)
        out_ref[chunk * group : (chunk + 1) * group, :capacity, :] = packed.reshape(
            group, capacity, LANES
        ).astype(jnp.bfloat16)
    line = lax.broadcasted_iota(jnp.int32, (8, 1), 0)
    for chunk in range(devices * 8 // CHUNK):
        pick = one_hot(in_chunk(third, chunk), CHUNK)
        packed = jnp.dot(pick, rows, preferred_element_type=jnp.float32)
        for step in range(CHUNK // 8):
            device = chunk * CHUNK // 8 + step
            block = packed[step * 8 : step * 8 + 8]
            block = jnp.where(line == 0, main_line[device : device + 1], block)
            block = jnp.where(line == 1, spare_line[device : device + 1], block)
            out_ref[device, capacity:, :] = block.astype(jnp.bfloat16)


def ordered_chunks(arrived_ref, flag_ref, count, capacity):
    devices = arrived_ref.shape[0]
    share = LANES // capacity
    lane = lax.broadcasted_iota(jnp.int32, (8, LANES), 1)
    tails = [arrived_ref[d, capacity:, :].astype(jnp.float32) for d in range(devices)]
    highs, lows, spares = [], [], []
    for first in range(0, devices, share):
        high = low = None
        for step in range(share):
            turned = step * capacity
            left = pltpu.roll(tails[first + step], turned, 1) if turned else tails[first + step]
            right = pltpu.roll(tails[first + step], (turned - capacity) % LANES, 1)
            if step:
                left = jnp.where(lane >= turned, left, high)
                right = jnp.where(lane >= turned, right, low)
            high, low = left, right
        highs.append(high[0:1])
        lows.append(low[0:1])
    for first in range(0, devices, LANES // 8):
        total = tails[first]
        for step in range(1, LANES // 8):
            total = total + tails[first + step]
        spares.append(total[1:2])
    high = jnp.concatenate(highs, axis=1)
    low = jnp.concatenate(lows, axis=1)
    spare = jnp.concatenate(spares, axis=1)
    flag_ref[0] = (jnp.max(spare) >= LOST).astype(jnp.int32)
    rows = arrived_ref[:, :capacity, :].reshape(devices * capacity, LANES)
    for chunk in range(count // CHUNK):
        pick = one_hot(jnp.where(high == chunk + 1, low, -1.0), CHUNK)
        yield jnp.dot(pick, rows, preferred_element_type=jnp.float32)
    pick = one_hot(jnp.where(high == count // CHUNK + 1, low, -1.0), WIN)
    others = jnp.concatenate(tails, axis=0).astype(jnp.bfloat16)
    yield jnp.dot(pick, rows, preferred_element_type=jnp.float32) + jnp.dot(
        one_hot(spare - 1.0, WIN), others, preferred_element_type=jnp.float32
    )


def turn_tail(rows):
    padding = jnp.zeros((LANES - rows.shape[0], LANES), jnp.float32)
    return jnp.concatenate([rows, padding], axis=0).T


def prepare_kernel(weight_ref, bias_ref, score_ref, turned_ref, floor_ref, scale_ref, base_ref):
    turned_ref[...] = weight_ref[...].astype(jnp.float32).T.astype(jnp.bfloat16)
    bias = bias_ref[...]
    score = score_ref[...].astype(jnp.float32)
    hidden = bias.shape[1]
    floor = jnp.broadcast_to(-bias, (CHUNK, hidden)).T
    floor_ref[...] = floor
    scale_ref[...] = jnp.broadcast_to(score, (CHUNK, hidden)).T
    base_ref[...] = jnp.broadcast_to(
        jnp.sum(bias * score, axis=1, keepdims=True), base_ref.shape
    )


def score_block(columns, write, turned_ref, floor_ref, scale_ref, base_ref):
    columns = columns.astype(jnp.bfloat16)
    leading = columns[:, :CHUNK]
    weight = turned_ref[...]
    for offset in range(1, WIN):
        partner = pltpu.roll(columns, columns.shape[1] - offset, 1)[:, :CHUNK]
        features = jnp.concatenate(
            [leading * partner, jnp.abs(leading - partner)], axis=0
        )
        hidden = jnp.dot(weight, features, preferred_element_type=jnp.float32)
        hidden = jnp.maximum(hidden, floor_ref[...]) * scale_ref[...]
        write(offset, jnp.sum(hidden, axis=0, keepdims=True) + base_ref[...])


def score_last(columns, limit, base, out_ref, parameters):
    place = base + lax.broadcasted_iota(jnp.int32, (1, CHUNK), 1)

    def write(offset, line):
        out_ref[offset - 1 : offset, :] = jnp.where(place + offset < limit, line, 0.0)

    score_block(columns, write, *parameters)


def main_kernel(limit_ref, arrived_ref, *refs, capacity):
    parameters = refs[:4]
    out_ref, last_ref, head_ref, flag_ref, wide_ref, scores_ref, sems = refs[4:]
    count = out_ref.shape[1]
    blocks = count // CHUNK
    for chunk, ordered in enumerate(ordered_chunks(arrived_ref, flag_ref, count, capacity)):
        if chunk < blocks:
            wide_ref[:, chunk * CHUNK : (chunk + 1) * CHUNK] = ordered.T
        else:
            wide_ref[:, count:] = turn_tail(ordered)
        if chunk == 0:
            head_ref[...] = ordered[: head_ref.shape[0]].astype(jnp.bfloat16)
    last_ref[...] = wide_ref[:, count - CHUNK : count]
    copies = []
    for block in range(blocks):
        start = block * CHUNK
        columns = wide_ref[:, start : start + CHUNK + LANES]
        place_ref = scores_ref.at[block]
        if block < blocks - 1:

            def write(offset, line, place_ref=place_ref):
                place_ref[offset - 1 : offset, :] = line

            score_block(columns, write, *parameters)
        else:
            score_last(columns, limit_ref[0], start, place_ref, parameters)
        copies.append(
            pltpu.make_async_copy(
                place_ref, out_ref.at[:, start : start + CHUNK], sems.at[block]
            )
        )
        copies[-1].start()
    for copy in copies:
        copy.wait()


def repair_kernel(limit_ref, last_ref, next_ref, *refs):
    out_ref, scores_ref, sem = refs[5:]
    base = out_ref.shape[1] - CHUNK
    following = turn_tail(next_ref[...].astype(jnp.float32))
    columns = jnp.concatenate([last_ref[...], following], axis=1)
    score_last(columns, limit_ref[0], base, scores_ref, refs[:4])
    copy = pltpu.make_async_copy(scores_ref, out_ref.at[:, base:], sem)
    copy.start()
    copy.wait()


def body(embeddings, ranks, pair_weight, pair_bias, score_weight):
    rows_dev, width = embeddings.shape
    devices = lax.axis_size("dev")
    capacity = 2 * rows_dev // devices
    hidden = pair_weight.shape[1]

    me = lax.axis_index("dev")
    outgoing = pl.pallas_call(
        functools.partial(pack_kernel, devices=devices, capacity=capacity),
        out_shape=jax.ShapeDtypeStruct((devices, capacity + 8, width), jnp.bfloat16),
        in_specs=[SMEM, ANY, ANY],
        out_specs=VMEM,
        scratch_shapes=[
            pltpu.VMEM((1, rows_dev), jnp.int32),
            pltpu.VMEM((rows_dev, width), jnp.bfloat16),
            pltpu.SemaphoreType.DMA((2,)),
        ],
        name="pack",
    )(me.astype(jnp.int32).reshape(1), ranks.reshape(1, rows_dev), embeddings)
    arrived = lax.all_to_all(outgoing, "dev", split_axis=0, concat_axis=0, tiled=True)
    parameters = pl.pallas_call(
        prepare_kernel,
        out_shape=(
            jax.ShapeDtypeStruct((hidden, 2 * width), jnp.bfloat16),
            jax.ShapeDtypeStruct((hidden, CHUNK), jnp.float32),
            jax.ShapeDtypeStruct((hidden, CHUNK), jnp.float32),
            jax.ShapeDtypeStruct((1, CHUNK), jnp.float32),
        ),
        in_specs=[VMEM] * 3,
        out_specs=(VMEM,) * 4,
        compiler_params=SMALL,
        name="prepare",
    )(pair_weight, pair_bias.reshape(1, hidden), score_weight.reshape(1, hidden))

    limit = jnp.where(me == devices - 1, rows_dev, 2 * rows_dev).astype(jnp.int32).reshape(1)
    scores, last, head, lost = pl.pallas_call(
        functools.partial(main_kernel, capacity=capacity),
        out_shape=(
            jax.ShapeDtypeStruct((WIN - 1, rows_dev), jnp.float32),
            jax.ShapeDtypeStruct((width, CHUNK), jnp.float32),
            jax.ShapeDtypeStruct((WIN, width), jnp.bfloat16),
            jax.ShapeDtypeStruct((1,), jnp.int32),
        ),
        in_specs=[SMEM] + [VMEM] * 5,
        out_specs=(HBM, VMEM, VMEM, SMEM),
        scratch_shapes=[
            pltpu.VMEM((width, rows_dev + LANES), jnp.float32),
            pltpu.VMEM((rows_dev // CHUNK, WIN - 1, CHUNK), jnp.float32),
            pltpu.SemaphoreType.DMA((rows_dev // CHUNK,)),
        ],
        compiler_params=SMALL,
        name="main",
    )(limit, arrived, *parameters)

    def repair(scores, limit, last, head, *parameters):
        following = lax.ppermute(head, "dev", [(i, i - 1) for i in range(1, devices)])
        return pl.pallas_call(
            repair_kernel,
            out_shape=jax.ShapeDtypeStruct(scores.shape, jnp.float32),
            in_specs=[SMEM] + [VMEM] * 6 + [HBM],
            out_specs=HBM,
            scratch_shapes=[
                pltpu.VMEM((WIN - 1, CHUNK), jnp.float32),
                pltpu.SemaphoreType.DMA,
            ],
            input_output_aliases={7: 0},
            compiler_params=SMALL,
            name="repair",
        )(limit, last, following, *parameters, scores)

    return lax.cond(
        lost[0] > 0,
        repair,
        lambda scores, *_: scores,
        scores, limit, last, head, *parameters,
    )


def solution(mesh):
    placed = (P("dev", None), P("dev"), P(), P(), P())
    return jax.shard_map(
        body, mesh=mesh, in_specs=placed, out_specs=P(None, "dev"), check_vma=False
    )
```

```python
import functools

import jax
import jax.numpy as jnp
from jax import lax
from jax.experimental import pallas as pl
from jax.experimental.pallas import tpu as pltpu
from jax.sharding import PartitionSpec as P

WIN = 32
LANES = 128
CHUNK = 256
SPARE = 6
LOST = 255.0
VMEM = pl.BlockSpec(memory_space=pltpu.VMEM)
SMEM = pl.BlockSpec(memory_space=pltpu.SMEM)
ANY = pl.BlockSpec(memory_space=pl.ANY)
HBM = pl.BlockSpec(memory_space=pltpu.HBM)
SMALL = pltpu.CompilerParams(vmem_limit_bytes=16 * 2**20)


def matches(values, count):
    index = lax.broadcasted_iota(jnp.int32, (count, 1), 0).astype(jnp.float32)
    return values.astype(jnp.bfloat16) == index.astype(jnp.bfloat16)


def one_hot(values, count):
    return jnp.where(matches(values, count), jnp.bfloat16(1), jnp.bfloat16(0))


def in_chunk(values, chunk):
    local = values - chunk * CHUNK
    return jnp.where((local >= 0) & (local < CHUNK), local, -1)


def pack_kernel(
    me_ref, ranks_hbm, rows_hbm, out_ref, ranks_ref, rows_ref, sems, *, devices, capacity
):
    ranks_copy = pltpu.make_async_copy(ranks_hbm, ranks_ref, sems.at[0])
    rows_copy = pltpu.make_async_copy(rows_hbm, rows_ref, sems.at[1])
    ranks_copy.start()
    rows_copy.start()
    count = rows_ref.shape[0]
    ranks_copy.wait()
    ranks = ranks_ref[...]
    owner = ranks // count
    position = ranks - owner * count
    before_owner = jnp.where(position < WIN - 1, owner, 0) - 1

    device_ids = lax.broadcasted_iota(jnp.int32, (devices, 1), 0)
    before = (
        lax.broadcasted_iota(jnp.int32, (CHUNK, CHUNK), 0)
        < lax.broadcasted_iota(jnp.int32, (CHUNK, CHUNK), 1)
    )
    before = jnp.where(before, 1.0, 0.0).astype(jnp.bfloat16)
    totals = jnp.zeros((2 * devices, 1), jnp.float32)
    members, indices = [], []
    for start in range(0, count, CHUNK):
        span = slice(start, start + CHUNK)
        member = jnp.concatenate(
            [
                jnp.where(device_ids == owner[:, span], 1.0, 0.0),
                jnp.where(device_ids == before_owner[:, span], 1.0, 0.0),
            ],
            axis=0,
        )
        earlier = jnp.dot(
            member.astype(jnp.bfloat16), before, preferred_element_type=jnp.float32
        )
        members.append(member)
        indices.append(earlier + totals)
        totals = totals + jnp.sum(member, axis=1, keepdims=True)
    owned = totals[:devices]
    slot = jnp.concatenate(
        [
            jnp.sum(m[:devices] * i[:devices], axis=0, keepdims=True)
            for m, i in zip(members, indices)
        ],
        axis=1,
    ).astype(jnp.int32)
    again = jnp.concatenate(
        [
            jnp.sum(m[devices:] * (i[devices:] + owned), axis=0, keepdims=True)
            for m, i in zip(members, indices)
        ],
        axis=1,
    ).astype(jnp.int32)
    extra = before_owner >= 0
    fits = extra & (again < capacity)
    spare = extra & (again >= capacity) & (again < capacity + SPARE)
    lost = jnp.where(extra & (again >= capacity + SPARE), 1.0, 0.0)
    target = owner * capacity + slot
    second = jnp.where(fits, before_owner * capacity + again, -1)
    third = jnp.where(spare, before_owner * 8 + (again - capacity + 8 - SPARE), -1)

    high = (position // CHUNK + 1).astype(jnp.float32)
    low = (position % CHUNK).astype(jnp.float32)
    head = position.astype(jnp.float32)
    lane = lax.broadcasted_iota(jnp.int32, (LANES, 1), 0)
    corner = (me_ref[0] % (LANES // 8)) * 8
    spot = jnp.where(slot == lane % capacity, 1.0, 0.0).astype(jnp.bfloat16)
    where_again = jnp.where(
        fits, again, jnp.where(spare, LANES + corner + again - capacity + 8 - SPARE, -1)
    )
    spot_again = jnp.where(
        (where_again == lane % capacity) | (where_again == LANES + lane), 1.0, 0.0
    ).astype(jnp.bfloat16)
    mine = device_ids == owner
    theirs = device_ids == before_owner
    values = jnp.concatenate(
        [
            jnp.where(mine, high, 0.0),
            jnp.where(mine, low, 0.0),
            jnp.zeros((devices, count), jnp.float32),
        ],
        axis=0,
    ).astype(jnp.bfloat16)
    values_again = jnp.concatenate(
        [
            jnp.where(theirs & fits, jnp.float32(count // CHUNK + 1), 0.0),
            jnp.where(theirs & fits, head, 0.0),
            jnp.where(theirs & spare, head + 1.0, 0.0),
        ],
        axis=0,
    ).astype(jnp.bfloat16)
    contract = (((1,), (1,)), ((), ()))
    places = lax.dot_general(
        values, spot, contract, preferred_element_type=jnp.float32
    ) + lax.dot_general(
        values_again, spot_again, contract, preferred_element_type=jnp.float32
    )
    lane_row = lax.broadcasted_iota(jnp.int32, (1, LANES), 1)
    main_line = jnp.where(
        lane_row < capacity, places[:devices], places[devices : 2 * devices]
    )
    lost = jnp.max(lost, axis=1, keepdims=True)
    spare_line = places[2 * devices :] + jnp.where(lane_row == corner, LOST * lost, 0.0)

    rows_copy.wait()
    rows = rows_ref[...]
    group = CHUNK // capacity
    for chunk in range(devices * capacity // CHUNK):
        pick = jnp.where(
            matches(in_chunk(target, chunk), CHUNK) | matches(in_chunk(second, chunk), CHUNK),
            jnp.bfloat16(1),
            jnp.bfloat16(0),
        )
        packed = jnp.dot(pick, rows, preferred_element_type=jnp.float32)
        out_ref[chunk * group : (chunk + 1) * group, :capacity, :] = packed.reshape(
            group, capacity, LANES
        ).astype(jnp.bfloat16)
    line = lax.broadcasted_iota(jnp.int32, (8, 1), 0)
    for chunk in range(devices * 8 // CHUNK):
        pick = one_hot(in_chunk(third, chunk), CHUNK)
        packed = jnp.dot(pick, rows, preferred_element_type=jnp.float32)
        for step in range(CHUNK // 8):
            device = chunk * CHUNK // 8 + step
            block = packed[step * 8 : step * 8 + 8]
            block = jnp.where(line == 0, main_line[device : device + 1], block)
            block = jnp.where(line == 1, spare_line[device : device + 1], block)
            out_ref[device, capacity:, :] = block.astype(jnp.bfloat16)


def ordered_chunks(arrived_ref, flag_ref, count, capacity):
    devices = arrived_ref.shape[0]
    share = LANES // capacity
    lane = lax.broadcasted_iota(jnp.int32, (8, LANES), 1)
    tails = [arrived_ref[d, capacity:, :].astype(jnp.float32) for d in range(devices)]
    highs, lows, spares = [], [], []
    for first in range(0, devices, share):
        high = low = None
        for step in range(share):
            turned = step * capacity
            left = pltpu.roll(tails[first + step], turned, 1) if turned else tails[first + step]
            right = pltpu.roll(tails[first + step], (turned - capacity) % LANES, 1)
            if step:
                left = jnp.where(lane >= turned, left, high)
                right = jnp.where(lane >= turned, right, low)
            high, low = left, right
        highs.append(high[0:1])
        lows.append(low[0:1])
    for first in range(0, devices, LANES // 8):
        total = tails[first]
        for step in range(1, LANES // 8):
            total = total + tails[first + step]
        spares.append(total[1:2])
    high = jnp.concatenate(highs, axis=1)
    low = jnp.concatenate(lows, axis=1)
    spare = jnp.concatenate(spares, axis=1)
    flag_ref[0] = (jnp.max(spare) >= LOST).astype(jnp.int32)
    rows = arrived_ref[:, :capacity, :].reshape(devices * capacity, LANES)
    for chunk in range(count // CHUNK):
        pick = one_hot(jnp.where(high == chunk + 1, low, -1.0), CHUNK)
        yield jnp.dot(pick, rows, preferred_element_type=jnp.float32)
    pick = one_hot(jnp.where(high == count // CHUNK + 1, low, -1.0), WIN)
    others = jnp.concatenate(tails, axis=0).astype(jnp.bfloat16)
    yield jnp.dot(pick, rows, preferred_element_type=jnp.float32) + jnp.dot(
        one_hot(spare - 1.0, WIN), others, preferred_element_type=jnp.float32
    )


def turn_tail(rows):
    padding = jnp.zeros((LANES - rows.shape[0], LANES), jnp.float32)
    return jnp.concatenate([rows, padding], axis=0).T


def prepare_kernel(weight_ref, bias_ref, score_ref, turned_ref, floor_ref, scale_ref, base_ref):
    turned_ref[...] = weight_ref[...].astype(jnp.float32).T.astype(jnp.bfloat16)
    bias = bias_ref[...]
    score = score_ref[...].astype(jnp.float32)
    hidden = bias.shape[1]
    floor = jnp.broadcast_to(-bias, (CHUNK, hidden)).T
    floor_ref[...] = floor
    scale_ref[...] = jnp.broadcast_to(score, (CHUNK, hidden)).T
    base_ref[...] = jnp.broadcast_to(
        jnp.sum(bias * score, axis=1, keepdims=True), base_ref.shape
    )


def score_block(columns, write, turned_ref, floor_ref, scale_ref, base_ref):
    columns = columns.astype(jnp.bfloat16)
    leading = columns[:, :CHUNK]
    weight = turned_ref[...]
    for offset in range(1, WIN):
        partner = pltpu.roll(columns, columns.shape[1] - offset, 1)[:, :CHUNK]
        features = jnp.concatenate(
            [leading * partner, jnp.abs(leading - partner)], axis=0
        )
        hidden = jnp.dot(weight, features, preferred_element_type=jnp.float32)
        hidden = jnp.maximum(hidden, floor_ref[...]) * scale_ref[...]
        write(offset, jnp.sum(hidden, axis=0, keepdims=True) + base_ref[...])


def score_last(columns, limit, base, out_ref, parameters):
    place = base + lax.broadcasted_iota(jnp.int32, (1, CHUNK), 1)

    def write(offset, line):
        line = jnp.where(place + offset < limit, line, 0.0)
        out_ref[offset - 1 : offset, out_ref.shape[1] - CHUNK :] = line

    score_block(columns, write, *parameters)


def main_kernel(limit_ref, arrived_ref, *refs, capacity):
    parameters = refs[:4]
    out_ref, last_ref, head_ref, flag_ref, wide_ref, scores_ref, sem = refs[4:]
    count = out_ref.shape[1]
    blocks = count // CHUNK
    for chunk, ordered in enumerate(ordered_chunks(arrived_ref, flag_ref, count, capacity)):
        if chunk < blocks:
            wide_ref[:, chunk * CHUNK : (chunk + 1) * CHUNK] = ordered.T
        else:
            wide_ref[:, count:] = turn_tail(ordered)
        if chunk == 0:
            head_ref[...] = ordered[: head_ref.shape[0]].astype(jnp.bfloat16)
    last_ref[...] = wide_ref[:, count - CHUNK : count]
    for block in range(blocks):
        start = block * CHUNK
        columns = wide_ref[:, start : start + CHUNK + LANES]
        if block < blocks - 1:

            def write(offset, line, start=start):
                scores_ref[offset - 1 : offset, start : start + CHUNK] = line

            score_block(columns, write, *parameters)
        else:
            score_last(columns, limit_ref[0], start, scores_ref, parameters)
    copy = pltpu.make_async_copy(scores_ref, out_ref, sem)
    copy.start()
    copy.wait()


def repair_kernel(limit_ref, last_ref, next_ref, *refs):
    out_ref, scores_ref, sem = refs[5:]
    base = out_ref.shape[1] - CHUNK
    following = turn_tail(next_ref[...].astype(jnp.float32))
    columns = jnp.concatenate([last_ref[...], following], axis=1)
    score_last(columns, limit_ref[0], base, scores_ref, refs[:4])
    copy = pltpu.make_async_copy(scores_ref, out_ref.at[:, base:], sem)
    copy.start()
    copy.wait()


def body(embeddings, ranks, pair_weight, pair_bias, score_weight):
    rows_dev, width = embeddings.shape
    devices = lax.axis_size("dev")
    capacity = 2 * rows_dev // devices
    hidden = pair_weight.shape[1]

    me = lax.axis_index("dev")
    outgoing = pl.pallas_call(
        functools.partial(pack_kernel, devices=devices, capacity=capacity),
        out_shape=jax.ShapeDtypeStruct((devices, capacity + 8, width), jnp.bfloat16),
        in_specs=[SMEM, ANY, ANY],
        out_specs=VMEM,
        scratch_shapes=[
            pltpu.VMEM((1, rows_dev), jnp.int32),
            pltpu.VMEM((rows_dev, width), jnp.bfloat16),
            pltpu.SemaphoreType.DMA((2,)),
        ],
        name="pack",
    )(me.astype(jnp.int32).reshape(1), ranks.reshape(1, rows_dev), embeddings)
    arrived = lax.all_to_all(outgoing, "dev", split_axis=0, concat_axis=0, tiled=True)
    parameters = pl.pallas_call(
        prepare_kernel,
        out_shape=(
            jax.ShapeDtypeStruct((hidden, 2 * width), jnp.bfloat16),
            jax.ShapeDtypeStruct((hidden, CHUNK), jnp.float32),
            jax.ShapeDtypeStruct((hidden, CHUNK), jnp.float32),
            jax.ShapeDtypeStruct((1, CHUNK), jnp.float32),
        ),
        in_specs=[VMEM] * 3,
        out_specs=(VMEM,) * 4,
        compiler_params=SMALL,
        name="prepare",
    )(pair_weight, pair_bias.reshape(1, hidden), score_weight.reshape(1, hidden))

    limit = jnp.where(me == devices - 1, rows_dev, 2 * rows_dev).astype(jnp.int32).reshape(1)
    scores, last, head, lost = pl.pallas_call(
        functools.partial(main_kernel, capacity=capacity),
        out_shape=(
            pltpu.HBM((WIN - 1, rows_dev), jnp.float32),
            jax.ShapeDtypeStruct((width, CHUNK), jnp.float32),
            jax.ShapeDtypeStruct((WIN, width), jnp.bfloat16),
            pltpu.SMEM((1,), jnp.int32),
        ),
        in_specs=[SMEM] + [VMEM] * 5,
        out_specs=(HBM, VMEM, VMEM, SMEM),
        scratch_shapes=[
            pltpu.VMEM((width, rows_dev + LANES), jnp.float32),
            pltpu.VMEM((WIN - 1, rows_dev), jnp.float32),
            pltpu.SemaphoreType.DMA,
        ],
        compiler_params=pltpu.CompilerParams(
            vmem_limit_bytes=16 * 2**20,
        ),
        name="main",
    )(limit, arrived, *parameters)

    def repair(scores, limit, last, head, *parameters):
        following = lax.ppermute(head, "dev", [(i, i - 1) for i in range(1, devices)])
        return pl.pallas_call(
            repair_kernel,
            out_shape=pltpu.HBM(scores.shape, jnp.float32),
            in_specs=[SMEM] + [VMEM] * 6 + [HBM],
            out_specs=HBM,
            scratch_shapes=[
                pltpu.VMEM((WIN - 1, CHUNK), jnp.float32),
                pltpu.SemaphoreType.DMA,
            ],
            input_output_aliases={7: 0},
            compiler_params=SMALL,
            name="repair",
        )(limit, last, following, *parameters, scores)

    return lax.cond(
        lost[0] > 0,
        repair,
        lambda scores, *_: scores,
        scores, limit, last, head, *parameters,
    )


def solution(mesh):
    placed = (P("dev", None), P("dev"), P(), P(), P())
    return jax.shard_map(
        body, mesh=mesh, in_specs=placed, out_specs=P(None, "dev"), check_vma=False
    )
```

```python
import functools

import jax
import jax.numpy as jnp
from jax import lax
from jax.experimental import pallas as pl
from jax.experimental.pallas import tpu as pltpu
from jax.sharding import PartitionSpec as P

WIN = 32
LANES = 128
CHUNK = 256
SPARE = 6
LOST = 255.0
VMEM = pl.BlockSpec(memory_space=pltpu.VMEM)
SMEM = pl.BlockSpec(memory_space=pltpu.SMEM)
ANY = pl.BlockSpec(memory_space=pl.ANY)
HBM = pl.BlockSpec(memory_space=pltpu.HBM)
SMALL = pltpu.CompilerParams(vmem_limit_bytes=16 * 2**20)


def matches(values, count):
    index = lax.broadcasted_iota(jnp.int32, (count, 1), 0).astype(jnp.float32)
    return values.astype(jnp.bfloat16) == index.astype(jnp.bfloat16)


def one_hot(values, count):
    return jnp.where(matches(values, count), jnp.bfloat16(1), jnp.bfloat16(0))


def in_chunk(values, chunk):
    local = values - chunk * CHUNK
    return jnp.where((local >= 0) & (local < CHUNK), local, -1)


def pack_kernel(
    me_ref, ranks_hbm, rows_hbm, out_ref, ranks_ref, rows_ref, sems, *, devices, capacity
):
    ranks_copy = pltpu.make_async_copy(ranks_hbm, ranks_ref, sems.at[0])
    rows_copy = pltpu.make_async_copy(rows_hbm, rows_ref, sems.at[1])
    ranks_copy.start()
    rows_copy.start()
    count = rows_ref.shape[0]
    ranks_copy.wait()
    ranks = ranks_ref[...]
    owner = ranks // count
    position = ranks - owner * count
    before_owner = jnp.where(position < WIN - 1, owner, 0) - 1

    device_ids = lax.broadcasted_iota(jnp.int32, (devices, 1), 0)
    before = (
        lax.broadcasted_iota(jnp.int32, (CHUNK, CHUNK), 0)
        < lax.broadcasted_iota(jnp.int32, (CHUNK, CHUNK), 1)
    )
    before = jnp.where(before, 1.0, 0.0).astype(jnp.bfloat16)
    totals = jnp.zeros((2 * devices, 1), jnp.float32)
    members, indices = [], []
    for start in range(0, count, CHUNK):
        span = slice(start, start + CHUNK)
        member = jnp.concatenate(
            [
                jnp.where(device_ids == owner[:, span], 1.0, 0.0),
                jnp.where(device_ids == before_owner[:, span], 1.0, 0.0),
            ],
            axis=0,
        )
        earlier = jnp.dot(
            member.astype(jnp.bfloat16), before, preferred_element_type=jnp.float32
        )
        members.append(member)
        indices.append(earlier + totals)
        totals = totals + jnp.sum(member, axis=1, keepdims=True)
    owned = totals[:devices]
    slot = jnp.concatenate(
        [
            jnp.sum(m[:devices] * i[:devices], axis=0, keepdims=True)
            for m, i in zip(members, indices)
        ],
        axis=1,
    ).astype(jnp.int32)
    again = jnp.concatenate(
        [
            jnp.sum(m[devices:] * (i[devices:] + owned), axis=0, keepdims=True)
            for m, i in zip(members, indices)
        ],
        axis=1,
    ).astype(jnp.int32)
    extra = before_owner >= 0
    fits = extra & (again < capacity)
    spare = extra & (again >= capacity) & (again < capacity + SPARE)
    lost = jnp.where(extra & (again >= capacity + SPARE), 1.0, 0.0)
    target = owner * capacity + slot
    second = jnp.where(fits, before_owner * capacity + again, -1)
    third = jnp.where(spare, before_owner * 8 + (again - capacity + 8 - SPARE), -1)

    high = (position // CHUNK + 1).astype(jnp.float32)
    low = (position % CHUNK).astype(jnp.float32)
    head = position.astype(jnp.float32)
    lane = lax.broadcasted_iota(jnp.int32, (LANES, 1), 0)
    corner = (me_ref[0] % (LANES // 8)) * 8
    spot = jnp.where(slot == lane % capacity, 1.0, 0.0).astype(jnp.bfloat16)
    where_again = jnp.where(
        fits, again, jnp.where(spare, LANES + corner + again - capacity + 8 - SPARE, -1)
    )
    spot_again = jnp.where(
        (where_again == lane % capacity) | (where_again == LANES + lane), 1.0, 0.0
    ).astype(jnp.bfloat16)
    mine = device_ids == owner
    theirs = device_ids == before_owner
    values = jnp.concatenate(
        [
            jnp.where(mine, high, 0.0),
            jnp.where(mine, low, 0.0),
            jnp.zeros((devices, count), jnp.float32),
        ],
        axis=0,
    ).astype(jnp.bfloat16)
    values_again = jnp.concatenate(
        [
            jnp.where(theirs & fits, jnp.float32(count // CHUNK + 1), 0.0),
            jnp.where(theirs & fits, head, 0.0),
            jnp.where(theirs & spare, head + 1.0, 0.0),
        ],
        axis=0,
    ).astype(jnp.bfloat16)
    contract = (((1,), (1,)), ((), ()))
    places = lax.dot_general(
        values, spot, contract, preferred_element_type=jnp.float32
    ) + lax.dot_general(
        values_again, spot_again, contract, preferred_element_type=jnp.float32
    )
    lane_row = lax.broadcasted_iota(jnp.int32, (1, LANES), 1)
    main_line = jnp.where(
        lane_row < capacity, places[:devices], places[devices : 2 * devices]
    )
    lost = jnp.max(lost, axis=1, keepdims=True)
    spare_line = places[2 * devices :] + jnp.where(lane_row == corner, LOST * lost, 0.0)

    rows_copy.wait()
    rows = rows_ref[...]
    group = CHUNK // capacity
    for chunk in range(devices * capacity // CHUNK):
        pick = jnp.where(
            matches(in_chunk(target, chunk), CHUNK) | matches(in_chunk(second, chunk), CHUNK),
            jnp.bfloat16(1),
            jnp.bfloat16(0),
        )
        packed = jnp.dot(pick, rows, preferred_element_type=jnp.float32)
        out_ref[chunk * group : (chunk + 1) * group, :capacity, :] = packed.reshape(
            group, capacity, LANES
        ).astype(jnp.bfloat16)
    line = lax.broadcasted_iota(jnp.int32, (8, 1), 0)
    for chunk in range(devices * 8 // CHUNK):
        pick = one_hot(in_chunk(third, chunk), CHUNK)
        packed = jnp.dot(pick, rows, preferred_element_type=jnp.float32)
        for step in range(CHUNK // 8):
            device = chunk * CHUNK // 8 + step
            block = packed[step * 8 : step * 8 + 8]
            block = jnp.where(line == 0, main_line[device : device + 1], block)
            block = jnp.where(line == 1, spare_line[device : device + 1], block)
            out_ref[device, capacity:, :] = block.astype(jnp.bfloat16)


def ordered_chunks(arrived_ref, flag_ref, count, capacity):
    devices = arrived_ref.shape[0]
    share = LANES // capacity
    lane = lax.broadcasted_iota(jnp.int32, (8, LANES), 1)
    tails = [arrived_ref[d, capacity:, :].astype(jnp.float32) for d in range(devices)]
    highs, lows, spares = [], [], []
    for first in range(0, devices, share):
        high = low = None
        for step in range(share):
            turned = step * capacity
            left = pltpu.roll(tails[first + step], turned, 1) if turned else tails[first + step]
            right = pltpu.roll(tails[first + step], (turned - capacity) % LANES, 1)
            if step:
                left = jnp.where(lane >= turned, left, high)
                right = jnp.where(lane >= turned, right, low)
            high, low = left, right
        highs.append(high[0:1])
        lows.append(low[0:1])
    for first in range(0, devices, LANES // 8):
        total = tails[first]
        for step in range(1, LANES // 8):
            total = total + tails[first + step]
        spares.append(total[1:2])
    high = jnp.concatenate(highs, axis=1)
    low = jnp.concatenate(lows, axis=1)
    spare = jnp.concatenate(spares, axis=1)
    flag_ref[0] = (jnp.max(spare) >= LOST).astype(jnp.int32)
    rows = arrived_ref[:, :capacity, :].reshape(devices * capacity, LANES)
    for chunk in range(count // CHUNK):
        pick = one_hot(jnp.where(high == chunk + 1, low, -1.0), CHUNK)
        yield jnp.dot(pick, rows, preferred_element_type=jnp.float32)
    pick = one_hot(jnp.where(high == count // CHUNK + 1, low, -1.0), WIN)
    others = jnp.concatenate(tails, axis=0).astype(jnp.bfloat16)
    yield jnp.dot(pick, rows, preferred_element_type=jnp.float32) + jnp.dot(
        one_hot(spare - 1.0, WIN), others, preferred_element_type=jnp.float32
    )


def turn_tail(rows):
    padding = jnp.zeros((LANES - rows.shape[0], LANES), jnp.float32)
    return jnp.concatenate([rows, padding], axis=0).T


def prepare_kernel(weight_ref, bias_ref, score_ref, turned_ref, floor_ref, scale_ref, base_ref):
    turned_ref[...] = weight_ref[...].astype(jnp.float32).T.astype(jnp.bfloat16)
    bias = bias_ref[...]
    score = score_ref[...].astype(jnp.float32)
    hidden = bias.shape[1]
    floor = jnp.broadcast_to(-bias, (CHUNK, hidden)).T
    floor_ref[...] = floor
    scale_ref[...] = jnp.broadcast_to(score, (CHUNK, hidden)).T
    base_ref[...] = jnp.broadcast_to(
        jnp.sum(bias * score, axis=1, keepdims=True), base_ref.shape
    )


def score_block(columns, write, turned_ref, floor_ref, scale_ref, base_ref):
    leading = columns[:, :CHUNK]
    weight = turned_ref[...]
    for offset in range(1, WIN):
        partner = pltpu.roll(columns, columns.shape[1] - offset, 1)[:, :CHUNK]
        features = jnp.concatenate(
            [leading * partner, jnp.abs(leading - partner)], axis=0
        )
        hidden = jnp.dot(weight, features, preferred_element_type=jnp.float32)
        hidden = jnp.maximum(hidden, floor_ref[...]) * scale_ref[...]
        write(offset, jnp.sum(hidden, axis=0, keepdims=True) + base_ref[...])


def score_last(columns, limit, base, out_ref, parameters):
    place = base + lax.broadcasted_iota(jnp.int32, (1, CHUNK), 1)

    def write(offset, line):
        line = jnp.where(place + offset < limit, line, 0.0)
        out_ref[offset - 1 : offset, out_ref.shape[1] - CHUNK :] = line

    score_block(columns, write, *parameters)


def main_kernel(limit_ref, arrived_ref, *refs, capacity):
    parameters = refs[:4]
    out_ref, last_ref, head_ref, flag_ref, scores_ref, sem = refs[4:]
    count = out_ref.shape[1]
    blocks = count // CHUNK
    chunks = ordered_chunks(arrived_ref, flag_ref, count, capacity)

    turned = []

    def take(chunk):
        ordered = next(chunks)
        columns = ordered.T if chunk < blocks else turn_tail(ordered)
        if chunk == 0:
            head_ref[...] = ordered[: head_ref.shape[0]].astype(jnp.bfloat16)
        if chunk == blocks - 1:
            last_ref[...] = columns
        turned.append(columns.astype(jnp.bfloat16))

    for chunk in range(blocks + 1):
        take(chunk)
    for block in range(blocks):
        start = block * CHUNK
        columns = jnp.concatenate([turned[block], turned[block + 1][:, :LANES]], axis=1)
        if block < blocks - 1:

            def write(offset, line, start=start):
                scores_ref[offset - 1 : offset, start : start + CHUNK] = line

            score_block(columns, write, *parameters)
        else:
            score_last(columns, limit_ref[0], start, scores_ref, parameters)
    copy = pltpu.make_async_copy(scores_ref, out_ref, sem)
    copy.start()
    copy.wait()


def repair_kernel(limit_ref, last_ref, next_ref, *refs):
    out_ref, scores_ref, sem = refs[5:]
    base = out_ref.shape[1] - CHUNK
    following = turn_tail(next_ref[...].astype(jnp.float32))
    columns = jnp.concatenate([last_ref[...], following], axis=1).astype(jnp.bfloat16)
    score_last(columns, limit_ref[0], base, scores_ref, refs[:4])
    copy = pltpu.make_async_copy(scores_ref, out_ref.at[:, base:], sem)
    copy.start()
    copy.wait()


def body(embeddings, ranks, pair_weight, pair_bias, score_weight):
    rows_dev, width = embeddings.shape
    devices = lax.axis_size("dev")
    capacity = 2 * rows_dev // devices
    hidden = pair_weight.shape[1]

    me = lax.axis_index("dev")
    outgoing = pl.pallas_call(
        functools.partial(pack_kernel, devices=devices, capacity=capacity),
        out_shape=jax.ShapeDtypeStruct((devices, capacity + 8, width), jnp.bfloat16),
        in_specs=[SMEM, ANY, ANY],
        out_specs=VMEM,
        scratch_shapes=[
            pltpu.VMEM((1, rows_dev), jnp.int32),
            pltpu.VMEM((rows_dev, width), jnp.bfloat16),
            pltpu.SemaphoreType.DMA((2,)),
        ],
        name="pack",
    )(me.astype(jnp.int32).reshape(1), ranks.reshape(1, rows_dev), embeddings)
    arrived = lax.all_to_all(outgoing, "dev", split_axis=0, concat_axis=0, tiled=True)
    parameters = pl.pallas_call(
        prepare_kernel,
        out_shape=(
            jax.ShapeDtypeStruct((hidden, 2 * width), jnp.bfloat16),
            jax.ShapeDtypeStruct((hidden, CHUNK), jnp.float32),
            jax.ShapeDtypeStruct((hidden, CHUNK), jnp.float32),
            jax.ShapeDtypeStruct((1, CHUNK), jnp.float32),
        ),
        in_specs=[VMEM] * 3,
        out_specs=(VMEM,) * 4,
        compiler_params=SMALL,
        name="prepare",
    )(pair_weight, pair_bias.reshape(1, hidden), score_weight.reshape(1, hidden))

    limit = jnp.where(me == devices - 1, rows_dev, 2 * rows_dev).astype(jnp.int32).reshape(1)
    scores, last, head, lost = pl.pallas_call(
        functools.partial(main_kernel, capacity=capacity),
        out_shape=(
            pltpu.HBM((WIN - 1, rows_dev), jnp.float32),
            jax.ShapeDtypeStruct((width, CHUNK), jnp.float32),
            jax.ShapeDtypeStruct((WIN, width), jnp.bfloat16),
            pltpu.SMEM((1,), jnp.int32),
        ),
        in_specs=[SMEM] + [VMEM] * 5,
        out_specs=(HBM, VMEM, VMEM, SMEM),
        scratch_shapes=[
            pltpu.VMEM((WIN - 1, rows_dev), jnp.float32),
            pltpu.SemaphoreType.DMA,
        ],
        compiler_params=pltpu.CompilerParams(
            vmem_limit_bytes=16 * 2**20,
        ),
        name="main",
    )(limit, arrived, *parameters)

    def repair(scores, limit, last, head, *parameters):
        following = lax.ppermute(head, "dev", [(i, i - 1) for i in range(1, devices)])
        return pl.pallas_call(
            repair_kernel,
            out_shape=pltpu.HBM(scores.shape, jnp.float32),
            in_specs=[SMEM] + [VMEM] * 6 + [HBM],
            out_specs=HBM,
            scratch_shapes=[
                pltpu.VMEM((WIN - 1, CHUNK), jnp.float32),
                pltpu.SemaphoreType.DMA,
            ],
            input_output_aliases={7: 0},
            compiler_params=SMALL,
            name="repair",
        )(limit, last, following, *parameters, scores)

    return lax.cond(
        lost[0] > 0,
        repair,
        lambda scores, *_: scores,
        scores, limit, last, head, *parameters,
    )


def solution(mesh):
    placed = (P("dev", None), P("dev"), P(), P(), P())
    return jax.shard_map(
        body, mesh=mesh, in_specs=placed, out_specs=P(None, "dev"), check_vma=False
    )
```

```python
import functools

import jax
import jax.numpy as jnp
from jax import lax
from jax.experimental import pallas as pl
from jax.experimental.pallas import tpu as pltpu
from jax.sharding import PartitionSpec as P

WIN = 32
LANES = 128
CHUNK = 256
SPARE = 6
LOST = 255.0
VMEM = pl.BlockSpec(memory_space=pltpu.VMEM)
SMEM = pl.BlockSpec(memory_space=pltpu.SMEM)
ANY = pl.BlockSpec(memory_space=pl.ANY)
HBM = pl.BlockSpec(memory_space=pltpu.HBM)
SMALL = pltpu.CompilerParams(vmem_limit_bytes=16 * 2**20)


def matches(values, count):
    index = lax.broadcasted_iota(jnp.int32, (count, 1), 0).astype(jnp.float32)
    return values.astype(jnp.bfloat16) == index.astype(jnp.bfloat16)


def one_hot(values, count):
    return jnp.where(matches(values, count), jnp.bfloat16(1), jnp.bfloat16(0))


def in_chunk(values, chunk):
    local = values - chunk * CHUNK
    return jnp.where((local >= 0) & (local < CHUNK), local, -1)


def pack_kernel(
    me_ref, ranks_hbm, rows_hbm, out_ref, ranks_ref, rows_ref, sems, *, devices, capacity
):
    ranks_copy = pltpu.make_async_copy(ranks_hbm, ranks_ref, sems.at[0])
    rows_copy = pltpu.make_async_copy(rows_hbm, rows_ref, sems.at[1])
    ranks_copy.start()
    rows_copy.start()
    count = rows_ref.shape[0]
    ranks_copy.wait()
    ranks = ranks_ref[...]
    owner = ranks // count
    position = ranks - owner * count
    before_owner = jnp.where(position < WIN - 1, owner, 0) - 1

    device_ids = lax.broadcasted_iota(jnp.int32, (devices, 1), 0)
    before = (
        lax.broadcasted_iota(jnp.int32, (CHUNK, CHUNK), 0)
        < lax.broadcasted_iota(jnp.int32, (CHUNK, CHUNK), 1)
    )
    before = jnp.where(before, 1.0, 0.0).astype(jnp.bfloat16)
    totals = jnp.zeros((2 * devices, 1), jnp.float32)
    members, indices = [], []
    for start in range(0, count, CHUNK):
        span = slice(start, start + CHUNK)
        member = jnp.concatenate(
            [
                jnp.where(device_ids == owner[:, span], 1.0, 0.0),
                jnp.where(device_ids == before_owner[:, span], 1.0, 0.0),
            ],
            axis=0,
        )
        earlier = jnp.dot(
            member.astype(jnp.bfloat16), before, preferred_element_type=jnp.float32
        )
        members.append(member)
        indices.append(earlier + totals)
        totals = totals + jnp.sum(member, axis=1, keepdims=True)
    owned = totals[:devices]
    slot = jnp.concatenate(
        [
            jnp.sum(m[:devices] * i[:devices], axis=0, keepdims=True)
            for m, i in zip(members, indices)
        ],
        axis=1,
    ).astype(jnp.int32)
    again = jnp.concatenate(
        [
            jnp.sum(m[devices:] * (i[devices:] + owned), axis=0, keepdims=True)
            for m, i in zip(members, indices)
        ],
        axis=1,
    ).astype(jnp.int32)
    extra = before_owner >= 0
    fits = extra & (again < capacity)
    spare = extra & (again >= capacity) & (again < capacity + SPARE)
    lost = jnp.where(extra & (again >= capacity + SPARE), 1.0, 0.0)
    target = owner * capacity + slot
    second = jnp.where(fits, before_owner * capacity + again, -1)
    third = jnp.where(spare, before_owner * 8 + (again - capacity + 8 - SPARE), -1)

    rows_copy.wait()
    high = (position // CHUNK + 1).astype(jnp.float32)
    low = (position % CHUNK).astype(jnp.float32)
    head = position.astype(jnp.float32)
    lane = lax.broadcasted_iota(jnp.int32, (LANES, 1), 0)
    corner = (me_ref[0] % (LANES // 8)) * 8
    spot = jnp.where(slot == lane % capacity, 1.0, 0.0).astype(jnp.bfloat16)
    where_again = jnp.where(
        fits, again, jnp.where(spare, LANES + corner + again - capacity + 8 - SPARE, -1)
    )
    spot_again = jnp.where(
        (where_again == lane % capacity) | (where_again == LANES + lane), 1.0, 0.0
    ).astype(jnp.bfloat16)
    mine = device_ids == owner
    theirs = device_ids == before_owner
    values = jnp.concatenate(
        [
            jnp.where(mine, high, 0.0),
            jnp.where(mine, low, 0.0),
            jnp.zeros((devices, count), jnp.float32),
        ],
        axis=0,
    ).astype(jnp.bfloat16)
    values_again = jnp.concatenate(
        [
            jnp.where(theirs & fits, jnp.float32(count // CHUNK + 1), 0.0),
            jnp.where(theirs & fits, head, 0.0),
            jnp.where(theirs & spare, head + 1.0, 0.0),
        ],
        axis=0,
    ).astype(jnp.bfloat16)
    contract = (((1,), (1,)), ((), ()))
    places = lax.dot_general(
        values, spot, contract, preferred_element_type=jnp.float32
    ) + lax.dot_general(
        values_again, spot_again, contract, preferred_element_type=jnp.float32
    )
    lane_row = lax.broadcasted_iota(jnp.int32, (1, LANES), 1)
    main_line = jnp.where(
        lane_row < capacity, places[:devices], places[devices : 2 * devices]
    )
    lost = jnp.max(lost, axis=1, keepdims=True)
    spare_line = places[2 * devices :] + jnp.where(lane_row == corner, LOST * lost, 0.0)

    rows = rows_ref[...]
    group = CHUNK // capacity
    for chunk in range(devices * capacity // CHUNK):
        pick = jnp.where(
            matches(in_chunk(target, chunk), CHUNK) | matches(in_chunk(second, chunk), CHUNK),
            jnp.bfloat16(1),
            jnp.bfloat16(0),
        )
        packed = jnp.dot(pick, rows, preferred_element_type=jnp.float32)
        out_ref[chunk * group : (chunk + 1) * group, :capacity, :] = packed.reshape(
            group, capacity, LANES
        ).astype(jnp.bfloat16)
    line = lax.broadcasted_iota(jnp.int32, (8, 1), 0)
    for chunk in range(devices * 8 // CHUNK):
        pick = one_hot(in_chunk(third, chunk), CHUNK)
        packed = jnp.dot(pick, rows, preferred_element_type=jnp.float32)
        for step in range(CHUNK // 8):
            device = chunk * CHUNK // 8 + step
            block = packed[step * 8 : step * 8 + 8]
            block = jnp.where(line == 0, main_line[device : device + 1], block)
            block = jnp.where(line == 1, spare_line[device : device + 1], block)
            out_ref[device, capacity:, :] = block.astype(jnp.bfloat16)


def ordered_chunks(arrived_ref, flag_ref, count, capacity):
    devices = arrived_ref.shape[0]
    share = LANES // capacity
    lane = lax.broadcasted_iota(jnp.int32, (8, LANES), 1)
    tails = [arrived_ref[d, capacity:, :].astype(jnp.float32) for d in range(devices)]
    highs, lows, spares = [], [], []
    for first in range(0, devices, share):
        high = low = None
        for step in range(share):
            turned = step * capacity
            left = pltpu.roll(tails[first + step], turned, 1) if turned else tails[first + step]
            right = pltpu.roll(tails[first + step], (turned - capacity) % LANES, 1)
            if step:
                left = jnp.where(lane >= turned, left, high)
                right = jnp.where(lane >= turned, right, low)
            high, low = left, right
        highs.append(high[0:1])
        lows.append(low[0:1])
    for first in range(0, devices, LANES // 8):
        total = tails[first]
        for step in range(1, LANES // 8):
            total = total + tails[first + step]
        spares.append(total[1:2])
    high = jnp.concatenate(highs, axis=1)
    low = jnp.concatenate(lows, axis=1)
    spare = jnp.concatenate(spares, axis=1)
    flag_ref[0] = (jnp.max(spare) >= LOST).astype(jnp.int32)
    rows = arrived_ref[:, :capacity, :].reshape(devices * capacity, LANES)
    for chunk in range(count // CHUNK):
        pick = one_hot(jnp.where(high == chunk + 1, low, -1.0), CHUNK)
        yield jnp.dot(pick, rows, preferred_element_type=jnp.float32)
    pick = one_hot(jnp.where(high == count // CHUNK + 1, low, -1.0), WIN)
    others = jnp.concatenate(tails, axis=0).astype(jnp.bfloat16)
    yield jnp.dot(pick, rows, preferred_element_type=jnp.float32) + jnp.dot(
        one_hot(spare - 1.0, WIN), others, preferred_element_type=jnp.float32
    )


def turn_tail(rows):
    padding = jnp.zeros((LANES - rows.shape[0], LANES), jnp.float32)
    return jnp.concatenate([rows, padding], axis=0).T


def prepare_kernel(weight_ref, bias_ref, score_ref, turned_ref, floor_ref, scale_ref, base_ref):
    turned_ref[...] = weight_ref[...].astype(jnp.float32).T.astype(jnp.bfloat16)
    bias = bias_ref[...]
    score = score_ref[...].astype(jnp.float32)
    hidden = bias.shape[1]
    floor = jnp.broadcast_to(-bias, (CHUNK, hidden)).T
    floor_ref[...] = floor
    scale_ref[...] = jnp.broadcast_to(score, (CHUNK, hidden)).T
    base_ref[...] = jnp.broadcast_to(
        jnp.sum(bias * score, axis=1, keepdims=True), base_ref.shape
    )


def score_block(columns, write, turned_ref, floor_ref, scale_ref, base_ref):
    leading = columns[:, :CHUNK]
    weight = turned_ref[...]
    for offset in range(1, WIN):
        partner = pltpu.roll(columns, columns.shape[1] - offset, 1)[:, :CHUNK]
        features = jnp.concatenate(
            [leading * partner, jnp.abs(leading - partner)], axis=0
        )
        hidden = jnp.dot(weight, features, preferred_element_type=jnp.float32)
        hidden = jnp.maximum(hidden, floor_ref[...]) * scale_ref[...]
        write(offset, jnp.sum(hidden, axis=0, keepdims=True) + base_ref[...])


def score_last(columns, limit, base, out_ref, parameters):
    place = base + lax.broadcasted_iota(jnp.int32, (1, CHUNK), 1)

    def write(offset, line):
        line = jnp.where(place + offset < limit, line, 0.0)
        out_ref[offset - 1 : offset, out_ref.shape[1] - CHUNK :] = line

    score_block(columns, write, *parameters)


def main_kernel(limit_ref, arrived_ref, *refs, capacity):
    parameters = refs[:4]
    out_ref, last_ref, head_ref, flag_ref, scores_ref, sem = refs[4:]
    count = out_ref.shape[1]
    blocks = count // CHUNK
    chunks = ordered_chunks(arrived_ref, flag_ref, count, capacity)

    turned = []

    def take(chunk):
        ordered = next(chunks)
        columns = ordered.T if chunk < blocks else turn_tail(ordered)
        if chunk == 0:
            head_ref[...] = ordered[: head_ref.shape[0]].astype(jnp.bfloat16)
        if chunk == blocks - 1:
            last_ref[...] = columns
        turned.append(columns.astype(jnp.bfloat16))

    for chunk in range(blocks + 1):
        take(chunk)
    for block in range(blocks):
        start = block * CHUNK
        columns = jnp.concatenate([turned[block], turned[block + 1][:, :LANES]], axis=1)
        if block < blocks - 1:

            def write(offset, line, start=start):
                scores_ref[offset - 1 : offset, start : start + CHUNK] = line

            score_block(columns, write, *parameters)
        else:
            score_last(columns, limit_ref[0], start, scores_ref, parameters)
    copy = pltpu.make_async_copy(scores_ref, out_ref, sem)
    copy.start()
    copy.wait()


def repair_kernel(limit_ref, last_ref, next_ref, *refs):
    out_ref, scores_ref, sem = refs[5:]
    base = out_ref.shape[1] - CHUNK
    following = turn_tail(next_ref[...].astype(jnp.float32))
    columns = jnp.concatenate([last_ref[...], following], axis=1).astype(jnp.bfloat16)
    score_last(columns, limit_ref[0], base, scores_ref, refs[:4])
    copy = pltpu.make_async_copy(scores_ref, out_ref.at[:, base:], sem)
    copy.start()
    copy.wait()


def body(embeddings, ranks, pair_weight, pair_bias, score_weight):
    rows_dev, width = embeddings.shape
    devices = lax.axis_size("dev")
    capacity = 2 * rows_dev // devices
    hidden = pair_weight.shape[1]

    me = lax.axis_index("dev")
    outgoing = pl.pallas_call(
        functools.partial(pack_kernel, devices=devices, capacity=capacity),
        out_shape=jax.ShapeDtypeStruct((devices, capacity + 8, width), jnp.bfloat16),
        in_specs=[SMEM, ANY, ANY],
        out_specs=VMEM,
        scratch_shapes=[
            pltpu.VMEM((1, rows_dev), jnp.int32),
            pltpu.VMEM((rows_dev, width), jnp.bfloat16),
            pltpu.SemaphoreType.DMA((2,)),
        ],
        name="pack",
    )(me.astype(jnp.int32).reshape(1), ranks.reshape(1, rows_dev), embeddings)
    arrived = lax.all_to_all(outgoing, "dev", split_axis=0, concat_axis=0, tiled=True)
    parameters = pl.pallas_call(
        prepare_kernel,
        out_shape=(
            jax.ShapeDtypeStruct((hidden, 2 * width), jnp.bfloat16),
            jax.ShapeDtypeStruct((hidden, CHUNK), jnp.float32),
            jax.ShapeDtypeStruct((hidden, CHUNK), jnp.float32),
            jax.ShapeDtypeStruct((1, CHUNK), jnp.float32),
        ),
        in_specs=[VMEM] * 3,
        out_specs=(VMEM,) * 4,
        compiler_params=SMALL,
        name="prepare",
    )(pair_weight, pair_bias.reshape(1, hidden), score_weight.reshape(1, hidden))

    limit = jnp.where(me == devices - 1, rows_dev, 2 * rows_dev).astype(jnp.int32).reshape(1)
    scores, last, head, lost = pl.pallas_call(
        functools.partial(main_kernel, capacity=capacity),
        out_shape=(
            pltpu.HBM((WIN - 1, rows_dev), jnp.float32),
            jax.ShapeDtypeStruct((width, CHUNK), jnp.float32),
            jax.ShapeDtypeStruct((WIN, width), jnp.bfloat16),
            pltpu.SMEM((1,), jnp.int32),
        ),
        in_specs=[SMEM] + [VMEM] * 5,
        out_specs=(HBM, VMEM, VMEM, SMEM),
        scratch_shapes=[
            pltpu.VMEM((WIN - 1, rows_dev), jnp.float32),
            pltpu.SemaphoreType.DMA,
        ],
        compiler_params=pltpu.CompilerParams(
            vmem_limit_bytes=16 * 2**20,
        ),
        name="main",
    )(limit, arrived, *parameters)

    def repair(scores, limit, last, head, *parameters):
        following = lax.ppermute(head, "dev", [(i, i - 1) for i in range(1, devices)])
        return pl.pallas_call(
            repair_kernel,
            out_shape=pltpu.HBM(scores.shape, jnp.float32),
            in_specs=[SMEM] + [VMEM] * 6 + [HBM],
            out_specs=HBM,
            scratch_shapes=[
                pltpu.VMEM((WIN - 1, CHUNK), jnp.float32),
                pltpu.SemaphoreType.DMA,
            ],
            input_output_aliases={7: 0},
            compiler_params=SMALL,
            name="repair",
        )(limit, last, following, *parameters, scores)

    return lax.cond(
        lost[0] > 0,
        repair,
        lambda scores, *_: scores,
        scores, limit, last, head, *parameters,
    )


def solution(mesh):
    placed = (P("dev", None), P("dev"), P(), P(), P())
    return jax.shard_map(
        body, mesh=mesh, in_specs=placed, out_specs=P(None, "dev"), check_vma=False
    )
```

```python
import functools

import jax
import jax.numpy as jnp
from jax import lax
from jax.experimental import pallas as pl
from jax.experimental.pallas import tpu as pltpu
from jax.sharding import PartitionSpec as P

WIN = 32
LANES = 128
CHUNK = 256
SPARE = 6
LOST = 255.0
VMEM = pl.BlockSpec(memory_space=pltpu.VMEM)
SMEM = pl.BlockSpec(memory_space=pltpu.SMEM)
ANY = pl.BlockSpec(memory_space=pl.ANY)
HBM = pl.BlockSpec(memory_space=pltpu.HBM)
SMALL = pltpu.CompilerParams(vmem_limit_bytes=16 * 2**20)


def matches(values, count):
    index = lax.broadcasted_iota(jnp.int32, (count, 1), 0).astype(jnp.float32)
    return values.astype(jnp.bfloat16) == index.astype(jnp.bfloat16)


def one_hot(values, count):
    return jnp.where(matches(values, count), jnp.bfloat16(1), jnp.bfloat16(0))


def in_chunk(values, chunk):
    local = values - chunk * CHUNK
    return jnp.where((local >= 0) & (local < CHUNK), local, -1)


def pack_kernel(
    me_ref, ranks_hbm, rows_hbm, out_hbm, ranks_ref, rows_ref, out_ref, sems, *, devices, capacity
):
    ranks_copy = pltpu.make_async_copy(ranks_hbm, ranks_ref, sems.at[0])
    rows_copy = pltpu.make_async_copy(rows_hbm, rows_ref, sems.at[1])
    ranks_copy.start()
    rows_copy.start()
    count = rows_ref.shape[0]
    ranks_copy.wait()
    ranks = ranks_ref[...]
    owner = ranks // count
    position = ranks - owner * count
    before_owner = jnp.where(position < WIN - 1, owner, 0) - 1

    device_ids = lax.broadcasted_iota(jnp.int32, (devices, 1), 0)
    before = (
        lax.broadcasted_iota(jnp.int32, (CHUNK, CHUNK), 0)
        < lax.broadcasted_iota(jnp.int32, (CHUNK, CHUNK), 1)
    )
    before = jnp.where(before, 1.0, 0.0).astype(jnp.bfloat16)
    totals = jnp.zeros((2 * devices, 1), jnp.float32)
    members, indices = [], []
    for start in range(0, count, CHUNK):
        span = slice(start, start + CHUNK)
        member = jnp.concatenate(
            [
                jnp.where(device_ids == owner[:, span], 1.0, 0.0),
                jnp.where(device_ids == before_owner[:, span], 1.0, 0.0),
            ],
            axis=0,
        )
        earlier = jnp.dot(
            member.astype(jnp.bfloat16), before, preferred_element_type=jnp.float32
        )
        members.append(member)
        indices.append(earlier + totals)
        totals = totals + jnp.sum(member, axis=1, keepdims=True)
    owned = totals[:devices]
    slot = jnp.concatenate(
        [
            jnp.sum(m[:devices] * i[:devices], axis=0, keepdims=True)
            for m, i in zip(members, indices)
        ],
        axis=1,
    ).astype(jnp.int32)
    again = jnp.concatenate(
        [
            jnp.sum(m[devices:] * (i[devices:] + owned), axis=0, keepdims=True)
            for m, i in zip(members, indices)
        ],
        axis=1,
    ).astype(jnp.int32)
    extra = before_owner >= 0
    fits = extra & (again < capacity)
    spare = extra & (again >= capacity) & (again < capacity + SPARE)
    lost = jnp.where(extra & (again >= capacity + SPARE), 1.0, 0.0)
    target = owner * capacity + slot
    second = jnp.where(fits, before_owner * capacity + again, -1)
    third = jnp.where(spare, before_owner * 8 + (again - capacity + 8 - SPARE), -1)

    rows_copy.wait()
    high = (position // CHUNK + 1).astype(jnp.float32)
    low = (position % CHUNK).astype(jnp.float32)
    head = position.astype(jnp.float32)
    lane = lax.broadcasted_iota(jnp.int32, (LANES, 1), 0)
    corner = (me_ref[0] % (LANES // 8)) * 8
    spot = jnp.where(slot == lane % capacity, 1.0, 0.0).astype(jnp.bfloat16)
    where_again = jnp.where(
        fits, again, jnp.where(spare, LANES + corner + again - capacity + 8 - SPARE, -1)
    )
    spot_again = jnp.where(
        (where_again == lane % capacity) | (where_again == LANES + lane), 1.0, 0.0
    ).astype(jnp.bfloat16)
    mine = device_ids == owner
    theirs = device_ids == before_owner
    values = jnp.concatenate(
        [
            jnp.where(mine, high, 0.0),
            jnp.where(mine, low, 0.0),
            jnp.zeros((devices, count), jnp.float32),
        ],
        axis=0,
    ).astype(jnp.bfloat16)
    values_again = jnp.concatenate(
        [
            jnp.where(theirs & fits, jnp.float32(count // CHUNK + 1), 0.0),
            jnp.where(theirs & fits, head, 0.0),
            jnp.where(theirs & spare, head + 1.0, 0.0),
        ],
        axis=0,
    ).astype(jnp.bfloat16)
    contract = (((1,), (1,)), ((), ()))
    places = lax.dot_general(
        values, spot, contract, preferred_element_type=jnp.float32
    ) + lax.dot_general(
        values_again, spot_again, contract, preferred_element_type=jnp.float32
    )
    lane_row = lax.broadcasted_iota(jnp.int32, (1, LANES), 1)
    main_line = jnp.where(
        lane_row < capacity, places[:devices], places[devices : 2 * devices]
    )
    lost = jnp.max(lost, axis=1, keepdims=True)
    spare_line = places[2 * devices :] + jnp.where(lane_row == corner, LOST * lost, 0.0)

    rows = rows_ref[...]
    group = CHUNK // capacity
    line = lax.broadcasted_iota(jnp.int32, (8, 1), 0)
    for chunk in range(devices * 8 // CHUNK):
        pick = one_hot(in_chunk(third, chunk), CHUNK)
        packed = jnp.dot(pick, rows, preferred_element_type=jnp.float32)
        for step in range(CHUNK // 8):
            device = chunk * CHUNK // 8 + step
            block = packed[step * 8 : step * 8 + 8]
            block = jnp.where(line == 0, main_line[device : device + 1], block)
            block = jnp.where(line == 1, spare_line[device : device + 1], block)
            out_ref[device, capacity:, :] = block.astype(jnp.bfloat16)
    copies = []
    ends = {devices // 2: (0, devices // 2), devices: (devices // 2, devices)}
    for chunk in range(devices * capacity // CHUNK):
        pick = jnp.where(
            matches(in_chunk(target, chunk), CHUNK) | matches(in_chunk(second, chunk), CHUNK),
            jnp.bfloat16(1),
            jnp.bfloat16(0),
        )
        packed = jnp.dot(pick, rows, preferred_element_type=jnp.float32)
        out_ref[chunk * group : (chunk + 1) * group, :capacity, :] = packed.reshape(
            group, capacity, LANES
        ).astype(jnp.bfloat16)
        sent = ends.get((chunk + 1) * group)
        if sent:
            copies.append(
                pltpu.make_async_copy(
                    out_ref.at[slice(*sent)], out_hbm.at[slice(*sent)], sems.at[2 + len(copies)]
                )
            )
            copies[-1].start()
    for copy in copies:
        copy.wait()


def ordered_chunks(arrived_ref, flag_ref, count, capacity):
    devices = arrived_ref.shape[0]
    share = LANES // capacity
    lane = lax.broadcasted_iota(jnp.int32, (8, LANES), 1)
    tails = [arrived_ref[d, capacity:, :].astype(jnp.float32) for d in range(devices)]
    highs, lows, spares = [], [], []
    for first in range(0, devices, share):
        high = low = None
        for step in range(share):
            turned = step * capacity
            left = pltpu.roll(tails[first + step], turned, 1) if turned else tails[first + step]
            right = pltpu.roll(tails[first + step], (turned - capacity) % LANES, 1)
            if step:
                left = jnp.where(lane >= turned, left, high)
                right = jnp.where(lane >= turned, right, low)
            high, low = left, right
        highs.append(high[0:1])
        lows.append(low[0:1])
    for first in range(0, devices, LANES // 8):
        total = tails[first]
        for step in range(1, LANES // 8):
            total = total + tails[first + step]
        spares.append(total[1:2])
    high = jnp.concatenate(highs, axis=1)
    low = jnp.concatenate(lows, axis=1)
    spare = jnp.concatenate(spares, axis=1)
    flag_ref[0] = (jnp.max(spare) >= LOST).astype(jnp.int32)
    rows = arrived_ref[:, :capacity, :].reshape(devices * capacity, LANES)
    for chunk in range(count // CHUNK):
        pick = one_hot(jnp.where(high == chunk + 1, low, -1.0), CHUNK)
        yield jnp.dot(pick, rows, preferred_element_type=jnp.float32)
    pick = one_hot(jnp.where(high == count // CHUNK + 1, low, -1.0), WIN)
    others = jnp.concatenate(tails, axis=0).astype(jnp.bfloat16)
    yield jnp.dot(pick, rows, preferred_element_type=jnp.float32) + jnp.dot(
        one_hot(spare - 1.0, WIN), others, preferred_element_type=jnp.float32
    )


def turn_tail(rows):
    padding = jnp.zeros((LANES - rows.shape[0], LANES), jnp.float32)
    return jnp.concatenate([rows, padding], axis=0).T


def prepare_kernel(weight_ref, bias_ref, score_ref, turned_ref, floor_ref, scale_ref, base_ref):
    turned_ref[...] = weight_ref[...].astype(jnp.float32).T.astype(jnp.bfloat16)
    bias = bias_ref[...]
    score = score_ref[...].astype(jnp.float32)
    hidden = bias.shape[1]
    floor = jnp.broadcast_to(-bias, (CHUNK, hidden)).T
    floor_ref[...] = floor
    scale_ref[...] = jnp.broadcast_to(score, (CHUNK, hidden)).T
    base_ref[...] = jnp.broadcast_to(
        jnp.sum(bias * score, axis=1, keepdims=True), base_ref.shape
    )


def score_block(columns, write, turned_ref, floor_ref, scale_ref, base_ref):
    leading = columns[:, :CHUNK]
    weight = turned_ref[...]
    for offset in range(1, WIN):
        partner = pltpu.roll(columns, columns.shape[1] - offset, 1)[:, :CHUNK]
        features = jnp.concatenate(
            [leading * partner, jnp.abs(leading - partner)], axis=0
        )
        hidden = jnp.dot(weight, features, preferred_element_type=jnp.float32)
        hidden = jnp.maximum(hidden, floor_ref[...]) * scale_ref[...]
        write(offset, jnp.sum(hidden, axis=0, keepdims=True) + base_ref[...])


def score_last(columns, limit, base, out_ref, parameters):
    place = base + lax.broadcasted_iota(jnp.int32, (1, CHUNK), 1)

    def write(offset, line):
        line = jnp.where(place + offset < limit, line, 0.0)
        out_ref[offset - 1 : offset, out_ref.shape[1] - CHUNK :] = line

    score_block(columns, write, *parameters)


def main_kernel(limit_ref, arrived_ref, *refs, capacity):
    parameters = refs[:4]
    out_ref, last_ref, head_ref, flag_ref, scores_ref, sem = refs[4:]
    count = out_ref.shape[1]
    blocks = count // CHUNK
    chunks = ordered_chunks(arrived_ref, flag_ref, count, capacity)

    turned = []

    def take(chunk):
        ordered = next(chunks)
        columns = ordered.T if chunk < blocks else turn_tail(ordered)
        if chunk == 0:
            head_ref[...] = ordered[: head_ref.shape[0]].astype(jnp.bfloat16)
        if chunk == blocks - 1:
            last_ref[...] = columns
        turned.append(columns.astype(jnp.bfloat16))

    for chunk in range(blocks + 1):
        take(chunk)
    for block in range(blocks):
        start = block * CHUNK
        columns = jnp.concatenate([turned[block], turned[block + 1][:, :LANES]], axis=1)
        if block < blocks - 1:

            def write(offset, line, start=start):
                scores_ref[offset - 1 : offset, start : start + CHUNK] = line

            score_block(columns, write, *parameters)
        else:
            score_last(columns, limit_ref[0], start, scores_ref, parameters)
    copy = pltpu.make_async_copy(scores_ref, out_ref, sem)
    copy.start()
    copy.wait()


def repair_kernel(limit_ref, last_ref, next_ref, *refs):
    out_ref, scores_ref, sem = refs[5:]
    base = out_ref.shape[1] - CHUNK
    following = turn_tail(next_ref[...].astype(jnp.float32))
    columns = jnp.concatenate([last_ref[...], following], axis=1).astype(jnp.bfloat16)
    score_last(columns, limit_ref[0], base, scores_ref, refs[:4])
    copy = pltpu.make_async_copy(scores_ref, out_ref.at[:, base:], sem)
    copy.start()
    copy.wait()


def body(embeddings, ranks, pair_weight, pair_bias, score_weight):
    rows_dev, width = embeddings.shape
    devices = lax.axis_size("dev")
    capacity = 2 * rows_dev // devices
    hidden = pair_weight.shape[1]

    me = lax.axis_index("dev")
    outgoing = pl.pallas_call(
        functools.partial(pack_kernel, devices=devices, capacity=capacity),
        out_shape=jax.ShapeDtypeStruct((devices, capacity + 8, width), jnp.bfloat16),
        in_specs=[SMEM, ANY, ANY],
        out_specs=ANY,
        scratch_shapes=[
            pltpu.VMEM((1, rows_dev), jnp.int32),
            pltpu.VMEM((rows_dev, width), jnp.bfloat16),
            pltpu.VMEM((devices, capacity + 8, width), jnp.bfloat16),
            pltpu.SemaphoreType.DMA((4,)),
        ],
        name="pack",
    )(me.astype(jnp.int32).reshape(1), ranks.reshape(1, rows_dev), embeddings)
    arrived = lax.all_to_all(outgoing, "dev", split_axis=0, concat_axis=0, tiled=True)
    parameters = pl.pallas_call(
        prepare_kernel,
        out_shape=(
            jax.ShapeDtypeStruct((hidden, 2 * width), jnp.bfloat16),
            jax.ShapeDtypeStruct((hidden, CHUNK), jnp.float32),
            jax.ShapeDtypeStruct((hidden, CHUNK), jnp.float32),
            jax.ShapeDtypeStruct((1, CHUNK), jnp.float32),
        ),
        in_specs=[VMEM] * 3,
        out_specs=(VMEM,) * 4,
        compiler_params=SMALL,
        name="prepare",
    )(pair_weight, pair_bias.reshape(1, hidden), score_weight.reshape(1, hidden))

    limit = jnp.where(me == devices - 1, rows_dev, 2 * rows_dev).astype(jnp.int32).reshape(1)
    scores, last, head, lost = pl.pallas_call(
        functools.partial(main_kernel, capacity=capacity),
        out_shape=(
            pltpu.HBM((WIN - 1, rows_dev), jnp.float32),
            jax.ShapeDtypeStruct((width, CHUNK), jnp.float32),
            jax.ShapeDtypeStruct((WIN, width), jnp.bfloat16),
            pltpu.SMEM((1,), jnp.int32),
        ),
        in_specs=[SMEM] + [VMEM] * 5,
        out_specs=(HBM, VMEM, VMEM, SMEM),
        scratch_shapes=[
            pltpu.VMEM((WIN - 1, rows_dev), jnp.float32),
            pltpu.SemaphoreType.DMA,
        ],
        compiler_params=pltpu.CompilerParams(
            vmem_limit_bytes=16 * 2**20,
        ),
        name="main",
    )(limit, arrived, *parameters)

    def repair(scores, limit, last, head, *parameters):
        following = lax.ppermute(head, "dev", [(i, i - 1) for i in range(1, devices)])
        return pl.pallas_call(
            repair_kernel,
            out_shape=pltpu.HBM(scores.shape, jnp.float32),
            in_specs=[SMEM] + [VMEM] * 6 + [HBM],
            out_specs=HBM,
            scratch_shapes=[
                pltpu.VMEM((WIN - 1, CHUNK), jnp.float32),
                pltpu.SemaphoreType.DMA,
            ],
            input_output_aliases={7: 0},
            compiler_params=SMALL,
            name="repair",
        )(limit, last, following, *parameters, scores)

    return lax.cond(
        lost[0] > 0,
        repair,
        lambda scores, *_: scores,
        scores, limit, last, head, *parameters,
    )


def solution(mesh):
    placed = (P("dev", None), P("dev"), P(), P(), P())
    return jax.shard_map(
        body, mesh=mesh, in_specs=placed, out_specs=P(None, "dev"), check_vma=False
    )
```

```python
import functools

import jax
import jax.numpy as jnp
from jax import lax
from jax.experimental import pallas as pl
from jax.experimental.pallas import tpu as pltpu
from jax.sharding import PartitionSpec as P

WIN = 32
LANES = 128
CHUNK = 256
SPARE = 6
LOST = 255.0
VMEM = pl.BlockSpec(memory_space=pltpu.VMEM)
SMEM = pl.BlockSpec(memory_space=pltpu.SMEM)
ANY = pl.BlockSpec(memory_space=pl.ANY)
HBM = pl.BlockSpec(memory_space=pltpu.HBM)
SMALL = pltpu.CompilerParams(vmem_limit_bytes=16 * 2**20)


def matches(values, count):
    index = lax.broadcasted_iota(jnp.int32, (count, 1), 0).astype(jnp.float32)
    return values.astype(jnp.bfloat16) == index.astype(jnp.bfloat16)


def one_hot(values, count):
    return jnp.where(matches(values, count), jnp.bfloat16(1), jnp.bfloat16(0))


def in_chunk(values, chunk):
    local = values - chunk * CHUNK
    return jnp.where((local >= 0) & (local < CHUNK), local, -1)


def pack_kernel(
    me_ref, ranks_hbm, rows_hbm, out_hbm, ranks_ref, rows_ref, out_ref, sems, *, devices, capacity
):
    ranks_copy = pltpu.make_async_copy(ranks_hbm, ranks_ref, sems.at[0])
    rows_copy = pltpu.make_async_copy(rows_hbm, rows_ref, sems.at[1])
    ranks_copy.start()
    rows_copy.start()
    count = rows_ref.shape[0]
    ranks_copy.wait()
    ranks = ranks_ref[...]
    owner = ranks // count
    position = ranks - owner * count
    before_owner = jnp.where(position < WIN - 1, owner, 0) - 1

    device_ids = lax.broadcasted_iota(jnp.int32, (devices, 1), 0)
    before = (
        lax.broadcasted_iota(jnp.int32, (CHUNK, CHUNK), 0)
        < lax.broadcasted_iota(jnp.int32, (CHUNK, CHUNK), 1)
    )
    before = jnp.where(before, 1.0, 0.0).astype(jnp.bfloat16)
    totals = jnp.zeros((2 * devices, 1), jnp.float32)
    members, indices = [], []
    for start in range(0, count, CHUNK):
        span = slice(start, start + CHUNK)
        member = jnp.concatenate(
            [
                jnp.where(device_ids == owner[:, span], 1.0, 0.0),
                jnp.where(device_ids == before_owner[:, span], 1.0, 0.0),
            ],
            axis=0,
        )
        earlier = jnp.dot(
            member.astype(jnp.bfloat16), before, preferred_element_type=jnp.float32
        )
        members.append(member)
        indices.append(earlier + totals)
        totals = totals + jnp.sum(member, axis=1, keepdims=True)
    owned = totals[:devices]
    slot = jnp.concatenate(
        [
            jnp.sum(m[:devices] * i[:devices], axis=0, keepdims=True)
            for m, i in zip(members, indices)
        ],
        axis=1,
    ).astype(jnp.int32)
    again = jnp.concatenate(
        [
            jnp.sum(m[devices:] * (i[devices:] + owned), axis=0, keepdims=True)
            for m, i in zip(members, indices)
        ],
        axis=1,
    ).astype(jnp.int32)
    extra = before_owner >= 0
    fits = extra & (again < capacity)
    spare = extra & (again >= capacity) & (again < capacity + SPARE)
    lost = jnp.where(extra & (again >= capacity + SPARE), 1.0, 0.0)
    target = owner * capacity + slot
    second = jnp.where(fits, before_owner * capacity + again, -1)
    third = jnp.where(spare, before_owner * 8 + (again - capacity + 8 - SPARE), -1)

    rows_copy.wait()
    high = (position // CHUNK + 1).astype(jnp.float32)
    low = (position % CHUNK).astype(jnp.float32)
    head = position.astype(jnp.float32)
    lane = lax.broadcasted_iota(jnp.int32, (LANES, 1), 0)
    corner = (me_ref[0] % (LANES // 8)) * 8
    spot = jnp.where(slot == lane % capacity, 1.0, 0.0).astype(jnp.bfloat16)
    where_again = jnp.where(
        fits, again, jnp.where(spare, LANES + corner + again - capacity + 8 - SPARE, -1)
    )
    spot_again = jnp.where(
        (where_again == lane % capacity) | (where_again == LANES + lane), 1.0, 0.0
    ).astype(jnp.bfloat16)
    mine = device_ids == owner
    theirs = device_ids == before_owner
    values = jnp.concatenate(
        [
            jnp.where(mine, high, 0.0),
            jnp.where(mine, low, 0.0),
            jnp.zeros((devices, count), jnp.float32),
        ],
        axis=0,
    ).astype(jnp.bfloat16)
    values_again = jnp.concatenate(
        [
            jnp.where(theirs & fits, jnp.float32(count // CHUNK + 1), 0.0),
            jnp.where(theirs & fits, head, 0.0),
            jnp.where(theirs & spare, head + 1.0, 0.0),
        ],
        axis=0,
    ).astype(jnp.bfloat16)
    contract = (((1,), (1,)), ((), ()))
    places = lax.dot_general(
        values, spot, contract, preferred_element_type=jnp.float32
    ) + lax.dot_general(
        values_again, spot_again, contract, preferred_element_type=jnp.float32
    )
    lane_row = lax.broadcasted_iota(jnp.int32, (1, LANES), 1)
    main_line = jnp.where(
        lane_row < capacity, places[:devices], places[devices : 2 * devices]
    )
    lost = jnp.max(lost, axis=1, keepdims=True)
    spare_line = places[2 * devices :] + jnp.where(lane_row == corner, LOST * lost, 0.0)

    rows = rows_ref[...]
    group = CHUNK // capacity
    line = lax.broadcasted_iota(jnp.int32, (8, 1), 0)
    for chunk in range(devices * 8 // CHUNK):
        pick = one_hot(in_chunk(third, chunk), CHUNK)
        packed = jnp.dot(pick, rows, preferred_element_type=jnp.float32)
        for step in range(CHUNK // 8):
            device = chunk * CHUNK // 8 + step
            block = packed[step * 8 : step * 8 + 8]
            block = jnp.where(line == 0, main_line[device : device + 1], block)
            block = jnp.where(line == 1, spare_line[device : device + 1], block)
            out_ref[device, capacity:, :] = block.astype(jnp.bfloat16)
    copies = []
    quarter = devices // 4
    ends = {i * quarter: ((i - 1) * quarter, i * quarter) for i in range(1, 5)}
    for chunk in range(devices * capacity // CHUNK):
        pick = jnp.where(
            matches(in_chunk(target, chunk), CHUNK) | matches(in_chunk(second, chunk), CHUNK),
            jnp.bfloat16(1),
            jnp.bfloat16(0),
        )
        packed = jnp.dot(pick, rows, preferred_element_type=jnp.float32)
        out_ref[chunk * group : (chunk + 1) * group, :capacity, :] = packed.reshape(
            group, capacity, LANES
        ).astype(jnp.bfloat16)
        sent = ends.get((chunk + 1) * group)
        if sent:
            copies.append(
                pltpu.make_async_copy(
                    out_ref.at[slice(*sent)], out_hbm.at[slice(*sent)], sems.at[2 + len(copies)]
                )
            )
            copies[-1].start()
    for copy in copies:
        copy.wait()


def ordered_chunks(arrived_ref, flag_ref, count, capacity):
    devices = arrived_ref.shape[0]
    share = LANES // capacity
    lane = lax.broadcasted_iota(jnp.int32, (8, LANES), 1)
    tails = [arrived_ref[d, capacity:, :].astype(jnp.float32) for d in range(devices)]
    highs, lows, spares = [], [], []
    for first in range(0, devices, share):
        high = low = None
        for step in range(share):
            turned = step * capacity
            left = pltpu.roll(tails[first + step], turned, 1) if turned else tails[first + step]
            right = pltpu.roll(tails[first + step], (turned - capacity) % LANES, 1)
            if step:
                left = jnp.where(lane >= turned, left, high)
                right = jnp.where(lane >= turned, right, low)
            high, low = left, right
        highs.append(high[0:1])
        lows.append(low[0:1])
    for first in range(0, devices, LANES // 8):
        total = tails[first]
        for step in range(1, LANES // 8):
            total = total + tails[first + step]
        spares.append(total[1:2])
    high = jnp.concatenate(highs, axis=1)
    low = jnp.concatenate(lows, axis=1)
    spare = jnp.concatenate(spares, axis=1)
    flag_ref[0] = (jnp.max(spare) >= LOST).astype(jnp.int32)
    rows = arrived_ref[:, :capacity, :].reshape(devices * capacity, LANES)
    for chunk in range(count // CHUNK):
        pick = one_hot(jnp.where(high == chunk + 1, low, -1.0), CHUNK)
        yield jnp.dot(pick, rows, preferred_element_type=jnp.float32)
    pick = one_hot(jnp.where(high == count // CHUNK + 1, low, -1.0), WIN)
    others = jnp.concatenate(tails, axis=0).astype(jnp.bfloat16)
    yield jnp.dot(pick, rows, preferred_element_type=jnp.float32) + jnp.dot(
        one_hot(spare - 1.0, WIN), others, preferred_element_type=jnp.float32
    )


def turn_tail(rows):
    padding = jnp.zeros((LANES - rows.shape[0], LANES), jnp.float32)
    return jnp.concatenate([rows, padding], axis=0).T


def prepare_kernel(weight_ref, bias_ref, score_ref, turned_ref, floor_ref, scale_ref, base_ref):
    turned_ref[...] = weight_ref[...].astype(jnp.float32).T.astype(jnp.bfloat16)
    bias = bias_ref[...]
    score = score_ref[...].astype(jnp.float32)
    hidden = bias.shape[1]
    floor = jnp.broadcast_to(-bias, (CHUNK, hidden)).T
    floor_ref[...] = floor
    scale_ref[...] = jnp.broadcast_to(score, (CHUNK, hidden)).T
    base_ref[...] = jnp.broadcast_to(
        jnp.sum(bias * score, axis=1, keepdims=True), base_ref.shape
    )


def score_block(columns, write, turned_ref, floor_ref, scale_ref, base_ref):
    leading = columns[:, :CHUNK]
    weight = turned_ref[...]
    for offset in range(1, WIN):
        partner = pltpu.roll(columns, columns.shape[1] - offset, 1)[:, :CHUNK]
        features = jnp.concatenate(
            [leading * partner, jnp.abs(leading - partner)], axis=0
        )
        hidden = jnp.dot(weight, features, preferred_element_type=jnp.float32)
        hidden = jnp.maximum(hidden, floor_ref[...]) * scale_ref[...]
        write(offset, jnp.sum(hidden, axis=0, keepdims=True) + base_ref[...])


def score_last(columns, limit, base, out_ref, parameters):
    place = base + lax.broadcasted_iota(jnp.int32, (1, CHUNK), 1)

    def write(offset, line):
        line = jnp.where(place + offset < limit, line, 0.0)
        out_ref[offset - 1 : offset, out_ref.shape[1] - CHUNK :] = line

    score_block(columns, write, *parameters)


def main_kernel(limit_ref, arrived_ref, *refs, capacity):
    parameters = refs[:4]
    out_ref, last_ref, head_ref, flag_ref, scores_ref, sem = refs[4:]
    count = out_ref.shape[1]
    blocks = count // CHUNK
    chunks = ordered_chunks(arrived_ref, flag_ref, count, capacity)

    turned = []

    def take(chunk):
        ordered = next(chunks)
        columns = ordered.T if chunk < blocks else turn_tail(ordered)
        if chunk == 0:
            head_ref[...] = ordered[: head_ref.shape[0]].astype(jnp.bfloat16)
        if chunk == blocks - 1:
            last_ref[...] = columns
        turned.append(columns.astype(jnp.bfloat16))

    for chunk in range(blocks + 1):
        take(chunk)
    for block in range(blocks):
        start = block * CHUNK
        columns = jnp.concatenate([turned[block], turned[block + 1][:, :LANES]], axis=1)
        if block < blocks - 1:

            def write(offset, line, start=start):
                scores_ref[offset - 1 : offset, start : start + CHUNK] = line

            score_block(columns, write, *parameters)
        else:
            score_last(columns, limit_ref[0], start, scores_ref, parameters)
    copy = pltpu.make_async_copy(scores_ref, out_ref, sem)
    copy.start()
    copy.wait()


def repair_kernel(limit_ref, last_ref, next_ref, *refs):
    out_ref, scores_ref, sem = refs[5:]
    base = out_ref.shape[1] - CHUNK
    following = turn_tail(next_ref[...].astype(jnp.float32))
    columns = jnp.concatenate([last_ref[...], following], axis=1).astype(jnp.bfloat16)
    score_last(columns, limit_ref[0], base, scores_ref, refs[:4])
    copy = pltpu.make_async_copy(scores_ref, out_ref.at[:, base:], sem)
    copy.start()
    copy.wait()


def body(embeddings, ranks, pair_weight, pair_bias, score_weight):
    rows_dev, width = embeddings.shape
    devices = lax.axis_size("dev")
    capacity = 2 * rows_dev // devices
    hidden = pair_weight.shape[1]

    me = lax.axis_index("dev")
    outgoing = pl.pallas_call(
        functools.partial(pack_kernel, devices=devices, capacity=capacity),
        out_shape=jax.ShapeDtypeStruct((devices, capacity + 8, width), jnp.bfloat16),
        in_specs=[SMEM, ANY, ANY],
        out_specs=ANY,
        scratch_shapes=[
            pltpu.VMEM((1, rows_dev), jnp.int32),
            pltpu.VMEM((rows_dev, width), jnp.bfloat16),
            pltpu.VMEM((devices, capacity + 8, width), jnp.bfloat16),
            pltpu.SemaphoreType.DMA((6,)),
        ],
        name="pack",
    )(me.astype(jnp.int32).reshape(1), ranks.reshape(1, rows_dev), embeddings)
    arrived = lax.all_to_all(outgoing, "dev", split_axis=0, concat_axis=0, tiled=True)
    parameters = pl.pallas_call(
        prepare_kernel,
        out_shape=(
            jax.ShapeDtypeStruct((hidden, 2 * width), jnp.bfloat16),
            jax.ShapeDtypeStruct((hidden, CHUNK), jnp.float32),
            jax.ShapeDtypeStruct((hidden, CHUNK), jnp.float32),
            jax.ShapeDtypeStruct((1, CHUNK), jnp.float32),
        ),
        in_specs=[VMEM] * 3,
        out_specs=(VMEM,) * 4,
        compiler_params=SMALL,
        name="prepare",
    )(pair_weight, pair_bias.reshape(1, hidden), score_weight.reshape(1, hidden))

    limit = jnp.where(me == devices - 1, rows_dev, 2 * rows_dev).astype(jnp.int32).reshape(1)
    scores, last, head, lost = pl.pallas_call(
        functools.partial(main_kernel, capacity=capacity),
        out_shape=(
            pltpu.HBM((WIN - 1, rows_dev), jnp.float32),
            jax.ShapeDtypeStruct((width, CHUNK), jnp.float32),
            jax.ShapeDtypeStruct((WIN, width), jnp.bfloat16),
            pltpu.SMEM((1,), jnp.int32),
        ),
        in_specs=[SMEM] + [VMEM] * 5,
        out_specs=(HBM, VMEM, VMEM, SMEM),
        scratch_shapes=[
            pltpu.VMEM((WIN - 1, rows_dev), jnp.float32),
            pltpu.SemaphoreType.DMA,
        ],
        compiler_params=pltpu.CompilerParams(
            vmem_limit_bytes=16 * 2**20,
        ),
        name="main",
    )(limit, arrived, *parameters)

    def repair(scores, limit, last, head, *parameters):
        following = lax.ppermute(head, "dev", [(i, i - 1) for i in range(1, devices)])
        return pl.pallas_call(
            repair_kernel,
            out_shape=pltpu.HBM(scores.shape, jnp.float32),
            in_specs=[SMEM] + [VMEM] * 6 + [HBM],
            out_specs=HBM,
            scratch_shapes=[
                pltpu.VMEM((WIN - 1, CHUNK), jnp.float32),
                pltpu.SemaphoreType.DMA,
            ],
            input_output_aliases={7: 0},
            compiler_params=SMALL,
            name="repair",
        )(limit, last, following, *parameters, scores)

    return lax.cond(
        lost[0] > 0,
        repair,
        lambda scores, *_: scores,
        scores, limit, last, head, *parameters,
    )


def solution(mesh):
    placed = (P("dev", None), P("dev"), P(), P(), P())
    return jax.shard_map(
        body, mesh=mesh, in_specs=placed, out_specs=P(None, "dev"), check_vma=False
    )
```

```python
import functools

import jax
import jax.numpy as jnp
from jax import lax
from jax.experimental import pallas as pl
from jax.experimental.pallas import tpu as pltpu
from jax.sharding import PartitionSpec as P

WIN = 32
LANES = 128
CHUNK = 256
SPARE = 6
LOST = 255.0
VMEM = pl.BlockSpec(memory_space=pltpu.VMEM)
SMEM = pl.BlockSpec(memory_space=pltpu.SMEM)
ANY = pl.BlockSpec(memory_space=pl.ANY)
HBM = pl.BlockSpec(memory_space=pltpu.HBM)
SMALL = pltpu.CompilerParams(vmem_limit_bytes=16 * 2**20)


def matches(values, count):
    index = lax.broadcasted_iota(jnp.int32, (count, 1), 0).astype(jnp.float32)
    return values.astype(jnp.bfloat16) == index.astype(jnp.bfloat16)


def one_hot(values, count):
    return jnp.where(matches(values, count), jnp.bfloat16(1), jnp.bfloat16(0))


def in_chunk(values, chunk):
    local = values - chunk * CHUNK
    return jnp.where((local >= 0) & (local < CHUNK), local, -1)


def pack_kernel(
    me_ref, ranks_hbm, rows_hbm, out_hbm, ranks_ref, rows_ref, out_ref, sems, *, devices, capacity
):
    ranks_copy = pltpu.make_async_copy(ranks_hbm, ranks_ref, sems.at[0])
    rows_copy = pltpu.make_async_copy(rows_hbm, rows_ref, sems.at[1])
    ranks_copy.start()
    rows_copy.start()
    count = rows_ref.shape[0]
    ranks_copy.wait()
    ranks = ranks_ref[...]
    owner = ranks // count
    position = ranks - owner * count
    before_owner = jnp.where(position < WIN - 1, owner, 0) - 1

    device_ids = lax.broadcasted_iota(jnp.int32, (devices, 1), 0)
    before = (
        lax.broadcasted_iota(jnp.int32, (CHUNK, CHUNK), 0)
        < lax.broadcasted_iota(jnp.int32, (CHUNK, CHUNK), 1)
    )
    before = jnp.where(before, 1.0, 0.0).astype(jnp.bfloat16)
    totals = jnp.zeros((2 * devices, 1), jnp.float32)
    members, indices = [], []
    for start in range(0, count, CHUNK):
        span = slice(start, start + CHUNK)
        member = jnp.concatenate(
            [
                jnp.where(device_ids == owner[:, span], 1.0, 0.0),
                jnp.where(device_ids == before_owner[:, span], 1.0, 0.0),
            ],
            axis=0,
        )
        earlier = jnp.dot(
            member.astype(jnp.bfloat16), before, preferred_element_type=jnp.float32
        )
        members.append(member)
        indices.append(earlier + totals)
        totals = totals + jnp.sum(member, axis=1, keepdims=True)
    owned = totals[:devices]
    slot = jnp.concatenate(
        [
            jnp.sum(m[:devices] * i[:devices], axis=0, keepdims=True)
            for m, i in zip(members, indices)
        ],
        axis=1,
    ).astype(jnp.int32)
    again = jnp.concatenate(
        [
            jnp.sum(m[devices:] * (i[devices:] + owned), axis=0, keepdims=True)
            for m, i in zip(members, indices)
        ],
        axis=1,
    ).astype(jnp.int32)
    extra = before_owner >= 0
    fits = extra & (again < capacity)
    spare = extra & (again >= capacity) & (again < capacity + SPARE)
    lost = jnp.where(extra & (again >= capacity + SPARE), 1.0, 0.0)
    target = owner * capacity + slot
    second = jnp.where(fits, before_owner * capacity + again, -1)
    third = jnp.where(spare, before_owner * 8 + (again - capacity + 8 - SPARE), -1)

    rows_copy.wait()
    high = (position // CHUNK + 1).astype(jnp.float32)
    low = (position % CHUNK).astype(jnp.float32)
    head = position.astype(jnp.float32)
    lane = lax.broadcasted_iota(jnp.int32, (LANES, 1), 0)
    corner = (me_ref[0] % (LANES // 8)) * 8
    spot = jnp.where(slot == lane % capacity, 1.0, 0.0).astype(jnp.bfloat16)
    where_again = jnp.where(
        fits, again, jnp.where(spare, LANES + corner + again - capacity + 8 - SPARE, -1)
    )
    spot_again = jnp.where(
        (where_again == lane % capacity) | (where_again == LANES + lane), 1.0, 0.0
    ).astype(jnp.bfloat16)
    mine = device_ids == owner
    theirs = device_ids == before_owner
    values = jnp.concatenate(
        [
            jnp.where(mine, high, 0.0),
            jnp.where(mine, low, 0.0),
            jnp.zeros((devices, count), jnp.float32),
        ],
        axis=0,
    ).astype(jnp.bfloat16)
    values_again = jnp.concatenate(
        [
            jnp.where(theirs & fits, jnp.float32(count // CHUNK + 1), 0.0),
            jnp.where(theirs & fits, head, 0.0),
            jnp.where(theirs & spare, head + 1.0, 0.0),
        ],
        axis=0,
    ).astype(jnp.bfloat16)
    contract = (((1,), (1,)), ((), ()))
    places = lax.dot_general(
        values, spot, contract, preferred_element_type=jnp.float32
    ) + lax.dot_general(
        values_again, spot_again, contract, preferred_element_type=jnp.float32
    )
    lane_row = lax.broadcasted_iota(jnp.int32, (1, LANES), 1)
    main_line = jnp.where(
        lane_row < capacity, places[:devices], places[devices : 2 * devices]
    )
    lost = jnp.max(lost, axis=1, keepdims=True)
    spare_line = places[2 * devices :] + jnp.where(lane_row == corner, LOST * lost, 0.0)

    rows = rows_ref[...]
    group = CHUNK // capacity
    line = lax.broadcasted_iota(jnp.int32, (8, 1), 0)
    for chunk in range(devices * 8 // CHUNK):
        pick = one_hot(in_chunk(third, chunk), CHUNK)
        packed = jnp.dot(pick, rows, preferred_element_type=jnp.float32)
        for step in range(CHUNK // 8):
            device = chunk * CHUNK // 8 + step
            block = packed[step * 8 : step * 8 + 8]
            block = jnp.where(line == 0, main_line[device : device + 1], block)
            block = jnp.where(line == 1, spare_line[device : device + 1], block)
            out_ref[device, capacity:, :] = block.astype(jnp.bfloat16)
    copies = []
    most = devices * 3 // 4
    ends = {most: (0, most), devices: (most, devices)}
    for chunk in range(devices * capacity // CHUNK):
        pick = jnp.where(
            matches(in_chunk(target, chunk), CHUNK) | matches(in_chunk(second, chunk), CHUNK),
            jnp.bfloat16(1),
            jnp.bfloat16(0),
        )
        packed = jnp.dot(pick, rows, preferred_element_type=jnp.float32)
        out_ref[chunk * group : (chunk + 1) * group, :capacity, :] = packed.reshape(
            group, capacity, LANES
        ).astype(jnp.bfloat16)
        sent = ends.get((chunk + 1) * group)
        if sent:
            copies.append(
                pltpu.make_async_copy(
                    out_ref.at[slice(*sent)], out_hbm.at[slice(*sent)], sems.at[2 + len(copies)]
                )
            )
            copies[-1].start()
    for copy in copies:
        copy.wait()


def ordered_chunks(arrived_ref, flag_ref, count, capacity):
    devices = arrived_ref.shape[0]
    share = LANES // capacity
    lane = lax.broadcasted_iota(jnp.int32, (8, LANES), 1)
    tails = [arrived_ref[d, capacity:, :].astype(jnp.float32) for d in range(devices)]
    highs, lows, spares = [], [], []
    for first in range(0, devices, share):
        high = low = None
        for step in range(share):
            turned = step * capacity
            left = pltpu.roll(tails[first + step], turned, 1) if turned else tails[first + step]
            right = pltpu.roll(tails[first + step], (turned - capacity) % LANES, 1)
            if step:
                left = jnp.where(lane >= turned, left, high)
                right = jnp.where(lane >= turned, right, low)
            high, low = left, right
        highs.append(high[0:1])
        lows.append(low[0:1])
    for first in range(0, devices, LANES // 8):
        total = tails[first]
        for step in range(1, LANES // 8):
            total = total + tails[first + step]
        spares.append(total[1:2])
    high = jnp.concatenate(highs, axis=1)
    low = jnp.concatenate(lows, axis=1)
    spare = jnp.concatenate(spares, axis=1)
    flag_ref[0] = (jnp.max(spare) >= LOST).astype(jnp.int32)
    rows = arrived_ref[:, :capacity, :].reshape(devices * capacity, LANES)
    for chunk in range(count // CHUNK):
        pick = one_hot(jnp.where(high == chunk + 1, low, -1.0), CHUNK)
        yield jnp.dot(pick, rows, preferred_element_type=jnp.float32)
    pick = one_hot(jnp.where(high == count // CHUNK + 1, low, -1.0), WIN)
    others = jnp.concatenate(tails, axis=0).astype(jnp.bfloat16)
    yield jnp.dot(pick, rows, preferred_element_type=jnp.float32) + jnp.dot(
        one_hot(spare - 1.0, WIN), others, preferred_element_type=jnp.float32
    )


def turn_tail(rows):
    padding = jnp.zeros((LANES - rows.shape[0], LANES), jnp.float32)
    return jnp.concatenate([rows, padding], axis=0).T


def prepare_kernel(weight_ref, bias_ref, score_ref, turned_ref, floor_ref, scale_ref, base_ref):
    turned_ref[...] = weight_ref[...].astype(jnp.float32).T.astype(jnp.bfloat16)
    bias = bias_ref[...]
    score = score_ref[...].astype(jnp.float32)
    hidden = bias.shape[1]
    floor = jnp.broadcast_to(-bias, (CHUNK, hidden)).T
    floor_ref[...] = floor
    scale_ref[...] = jnp.broadcast_to(score, (CHUNK, hidden)).T
    base_ref[...] = jnp.broadcast_to(
        jnp.sum(bias * score, axis=1, keepdims=True), base_ref.shape
    )


def score_block(columns, write, turned_ref, floor_ref, scale_ref, base_ref):
    leading = columns[:, :CHUNK]
    weight = turned_ref[...]
    for offset in range(1, WIN):
        partner = pltpu.roll(columns, columns.shape[1] - offset, 1)[:, :CHUNK]
        features = jnp.concatenate(
            [leading * partner, jnp.abs(leading - partner)], axis=0
        )
        hidden = jnp.dot(weight, features, preferred_element_type=jnp.float32)
        hidden = jnp.maximum(hidden, floor_ref[...]) * scale_ref[...]
        write(offset, jnp.sum(hidden, axis=0, keepdims=True) + base_ref[...])


def score_last(columns, limit, base, out_ref, parameters):
    place = base + lax.broadcasted_iota(jnp.int32, (1, CHUNK), 1)

    def write(offset, line):
        line = jnp.where(place + offset < limit, line, 0.0)
        out_ref[offset - 1 : offset, out_ref.shape[1] - CHUNK :] = line

    score_block(columns, write, *parameters)


def main_kernel(limit_ref, arrived_ref, *refs, capacity):
    parameters = refs[:4]
    out_ref, last_ref, head_ref, flag_ref, scores_ref, sem = refs[4:]
    count = out_ref.shape[1]
    blocks = count // CHUNK
    chunks = ordered_chunks(arrived_ref, flag_ref, count, capacity)

    turned = []

    def take(chunk):
        ordered = next(chunks)
        columns = ordered.T if chunk < blocks else turn_tail(ordered)
        if chunk == 0:
            head_ref[...] = ordered[: head_ref.shape[0]].astype(jnp.bfloat16)
        if chunk == blocks - 1:
            last_ref[...] = columns
        turned.append(columns.astype(jnp.bfloat16))

    for chunk in range(blocks + 1):
        take(chunk)
    for block in range(blocks):
        start = block * CHUNK
        columns = jnp.concatenate([turned[block], turned[block + 1][:, :LANES]], axis=1)
        if block < blocks - 1:

            def write(offset, line, start=start):
                scores_ref[offset - 1 : offset, start : start + CHUNK] = line

            score_block(columns, write, *parameters)
        else:
            score_last(columns, limit_ref[0], start, scores_ref, parameters)
    copy = pltpu.make_async_copy(scores_ref, out_ref, sem)
    copy.start()
    copy.wait()


def repair_kernel(limit_ref, last_ref, next_ref, *refs):
    out_ref, scores_ref, sem = refs[5:]
    base = out_ref.shape[1] - CHUNK
    following = turn_tail(next_ref[...].astype(jnp.float32))
    columns = jnp.concatenate([last_ref[...], following], axis=1).astype(jnp.bfloat16)
    score_last(columns, limit_ref[0], base, scores_ref, refs[:4])
    copy = pltpu.make_async_copy(scores_ref, out_ref.at[:, base:], sem)
    copy.start()
    copy.wait()


def body(embeddings, ranks, pair_weight, pair_bias, score_weight):
    rows_dev, width = embeddings.shape
    devices = lax.axis_size("dev")
    capacity = 2 * rows_dev // devices
    hidden = pair_weight.shape[1]

    me = lax.axis_index("dev")
    outgoing = pl.pallas_call(
        functools.partial(pack_kernel, devices=devices, capacity=capacity),
        out_shape=jax.ShapeDtypeStruct((devices, capacity + 8, width), jnp.bfloat16),
        in_specs=[SMEM, ANY, ANY],
        out_specs=ANY,
        scratch_shapes=[
            pltpu.VMEM((1, rows_dev), jnp.int32),
            pltpu.VMEM((rows_dev, width), jnp.bfloat16),
            pltpu.VMEM((devices, capacity + 8, width), jnp.bfloat16),
            pltpu.SemaphoreType.DMA((4,)),
        ],
        name="pack",
    )(me.astype(jnp.int32).reshape(1), ranks.reshape(1, rows_dev), embeddings)
    arrived = lax.all_to_all(outgoing, "dev", split_axis=0, concat_axis=0, tiled=True)
    parameters = pl.pallas_call(
        prepare_kernel,
        out_shape=(
            jax.ShapeDtypeStruct((hidden, 2 * width), jnp.bfloat16),
            jax.ShapeDtypeStruct((hidden, CHUNK), jnp.float32),
            jax.ShapeDtypeStruct((hidden, CHUNK), jnp.float32),
            jax.ShapeDtypeStruct((1, CHUNK), jnp.float32),
        ),
        in_specs=[VMEM] * 3,
        out_specs=(VMEM,) * 4,
        compiler_params=SMALL,
        name="prepare",
    )(pair_weight, pair_bias.reshape(1, hidden), score_weight.reshape(1, hidden))

    limit = jnp.where(me == devices - 1, rows_dev, 2 * rows_dev).astype(jnp.int32).reshape(1)
    scores, last, head, lost = pl.pallas_call(
        functools.partial(main_kernel, capacity=capacity),
        out_shape=(
            pltpu.HBM((WIN - 1, rows_dev), jnp.float32),
            jax.ShapeDtypeStruct((width, CHUNK), jnp.float32),
            jax.ShapeDtypeStruct((WIN, width), jnp.bfloat16),
            pltpu.SMEM((1,), jnp.int32),
        ),
        in_specs=[SMEM] + [VMEM] * 5,
        out_specs=(HBM, VMEM, VMEM, SMEM),
        scratch_shapes=[
            pltpu.VMEM((WIN - 1, rows_dev), jnp.float32),
            pltpu.SemaphoreType.DMA,
        ],
        compiler_params=pltpu.CompilerParams(
            vmem_limit_bytes=16 * 2**20,
        ),
        name="main",
    )(limit, arrived, *parameters)

    def repair(scores, limit, last, head, *parameters):
        following = lax.ppermute(head, "dev", [(i, i - 1) for i in range(1, devices)])
        return pl.pallas_call(
            repair_kernel,
            out_shape=pltpu.HBM(scores.shape, jnp.float32),
            in_specs=[SMEM] + [VMEM] * 6 + [HBM],
            out_specs=HBM,
            scratch_shapes=[
                pltpu.VMEM((WIN - 1, CHUNK), jnp.float32),
                pltpu.SemaphoreType.DMA,
            ],
            input_output_aliases={7: 0},
            compiler_params=SMALL,
            name="repair",
        )(limit, last, following, *parameters, scores)

    return lax.cond(
        lost[0] > 0,
        repair,
        lambda scores, *_: scores,
        scores, limit, last, head, *parameters,
    )


def solution(mesh):
    placed = (P("dev", None), P("dev"), P(), P(), P())
    return jax.shard_map(
        body, mesh=mesh, in_specs=placed, out_specs=P(None, "dev"), check_vma=False
    )
```
